512 devices in a mesh: pool: 32 (over z, x), tp: 16 (over y, core).
Axes of the slice: x: 4, y: 8, z: 8, core: 2. Of those that a mesh axis runs over, the one named last changes fastest.
Arguments:
- activations: bfloat16 [2, 256, 8192], P(None, None, 'tp'), may hold values from -6 to 6
- gate_matrix: bfloat16 [8192, 28672], P('tp', 'pool'), may hold values from -0.0625 to 0.0625
- up_weight: bfloat16 [8192, 28672], P('tp', 'pool'), may hold values from -0.0625 to 0.0625
- down_matrix: bfloat16 [28672, 8192], P('pool', 'tp'), may hold values from -0.03125 to 0.03125
- shrink_pages: bfloat16 [128, 64, 8192], P('pool', None, 'tp'), may hold values from -0.0625 to 0.0625
- expand_pages: bfloat16 [128, 64, 28672], P('pool', 'tp'), may hold values from -0.75 to 0.75
- row_adapter: int32 [2, 256], replicated, may hold values from 0 to 127, as said below
- page_table: int32 [128], replicated, may hold values from 0 to 127, as said below
Outputs:
- layer_out: bfloat16 [2, 256, 8192], P(None, None, 'tp')
The draws below stay inside these ranges and needn't reach their ends.
Inputs may be any that keep to these rules, and one draw needn't show every extreme that they name: `row_adapter`: in each micro-batch, the rows use at most 1 distinct adapter among those whose pages have the same owner, the owner of page g being g // 4 (so a micro-batch may use up to 32 adapters, one per owner). A permutation: adapter a is stored at page page_table[a].
All inputs are finite; a program needn't handle non-finite values.
Results may differ from the reference program's by a relative error of at most 0.0057.
Values may be sent and summed in bfloat16 or wider, within the bound.
A program may use at most 64 MiB of HBM per device.

```python
import math
import jax
import jax.numpy as jnp
from jax import lax

MODEL_WIDTH = 8192
FF = 28672
R = 64
ROWS = 256
MB = 2
PAGES = 4
CAP = 1
ADAPTERS = 128


def adapter_tables(key):
    base_key = jax.random.fold_in(key, 11)
    page_table = jax.random.permutation(jax.random.fold_in(base_key, 1), ADAPTERS).astype(jnp.int32)
    adapter_at = jnp.argsort(page_table, stable=True).astype(jnp.int32)
    owners = ADAPTERS // PAGES
    batch_ids = jnp.arange(MB, dtype=jnp.int32)
    first_page = page_table[0]
    last_page = page_table[ADAPTERS - 1]
    target_page = jnp.where(batch_ids == 0, last_page, first_page).astype(jnp.int32)
    target_owner = (target_page // PAGES).astype(jnp.int32)
    starts = jax.random.randint(jax.random.fold_in(base_key, 2), (MB, owners), 0, PAGES).astype(jnp.int32)
    owner_ids = jnp.arange(owners, dtype=jnp.int32)
    starts = jnp.where(owner_ids[None, :] == target_owner[:, None], (target_page % PAGES)[:, None], starts)
    offsets = (starts[:, :, None] + jnp.arange(CAP, dtype=jnp.int32)) % PAGES
    candidates = (owner_ids[None, :, None] * PAGES + offsets).reshape(MB, owners * CAP).astype(jnp.int32)
    live_owner = jax.random.randint(jax.random.fold_in(base_key, 3), (MB, owners), 0, 2) == 1
    live_owner = live_owner | (owner_ids[None, :] == target_owner[:, None])
    live_flat = jnp.repeat(live_owner, CAP, axis=1)
    cand_count = owners * CAP
    levels = jnp.power(2, jax.random.randint(jax.random.fold_in(base_key, 5), (MB, cand_count), 0, 4)).astype(jnp.int32)
    noise = jax.random.randint(jax.random.fold_in(base_key, 6), (MB, ROWS, cand_count), 0, 65536)
    scores = noise * levels[:, None, :] * cand_count + jnp.arange(cand_count, dtype=jnp.int32)
    scores = jnp.where(live_flat[:, None, :], scores, -1).astype(jnp.int32)
    picked = lax.top_k(scores, 1)[1]
    spread = jnp.broadcast_to(candidates[:, None, :], (MB, ROWS, cand_count))
    page_pick = jnp.take_along_axis(spread, picked, axis=2)[:, :, 0]
    page_pick = page_pick.at[0, 0].set(last_page)
    if MB > 1:
        page_pick = page_pick.at[MB - 1, 0].set(first_page)
    else:
        page_pick = page_pick.at[0, 1].set(first_page)
    row_adapter = jnp.take(adapter_at, page_pick.astype(jnp.int32), axis=0).astype(jnp.int32)
    return (page_table, row_adapter)


def draw_page_table(key, part):
    return adapter_tables(key)[0]


def draw_row_adapter(key, part):
    return adapter_tables(key)[1]


def shard_levels(key, dims, cuts, smallest, top_value):
    factor_of, own = 1.0, jax.random.fold_in(key, 6)
    for position, parts in cuts:
        heights = jnp.exp(jax.random.uniform(jax.random.fold_in(own, position), (parts,), jnp.float32, smallest / len(cuts), top_value / len(cuts)))
        factor_of = factor_of * jnp.repeat(heights, dims[position] // parts).reshape([-1 if axis == position else 1 for axis in range(len(dims))])
    return factor_of


def centred(own_key, shape, width, most, cuts=(), kind=jnp.bfloat16):
    values = width * jax.random.normal(own_key, shape, jnp.float32)
    if cuts:
        values = values * shard_levels(own_key, shape, cuts, -0.22, 0.18)
    return jnp.clip(values, -most, most).astype(kind)


def setup_inputs(seed: int = 0) -> dict:
    seeds = jax.random.split(jax.random.key(seed), 9)
    activations = centred(seeds[0], (MB, ROWS, MODEL_WIDTH), 1.0, 6.0, ((2, 16),))
    gate_matrix = centred(seeds[1], (MODEL_WIDTH, FF), MODEL_WIDTH ** -0.5, 0.0625, ((0, 16), (1, 32)))
    up_weight = centred(seeds[2], (MODEL_WIDTH, FF), MODEL_WIDTH ** -0.5, 0.0625, ((0, 16), (1, 32)))
    down_matrix = centred(seeds[3], (FF, MODEL_WIDTH), FF ** -0.5, 0.03125, ((0, 32), (1, 16)))
    shrink_pages = centred(seeds[4], (ADAPTERS, R, MODEL_WIDTH), MODEL_WIDTH ** -0.5, 0.0625, ((0, 32), (2, 16)))
    expand_pages = centred(seeds[5], (ADAPTERS, R, FF), R ** -0.5, 0.75, ((0, 32), (1, 16)))
    row_adapter = draw_row_adapter(jax.random.fold_in(seeds[8], 71), 0)
    page_table = draw_page_table(jax.random.fold_in(seeds[8], 71), 0)
    return dict(activations=activations, gate_matrix=gate_matrix, up_weight=up_weight, down_matrix=down_matrix, shrink_pages=shrink_pages, expand_pages=expand_pages, row_adapter=row_adapter, page_table=page_table)


adapter_scale = 2.0


def reference(activations, gate_matrix, up_weight, down_matrix, shrink_pages, expand_pages, row_adapter, page_table):
    catalog = jnp.arange(ADAPTERS, dtype=jnp.int32)
    page_of_row = jnp.sum(jnp.where(row_adapter[:, :, None] == catalog, page_table, 0), axis=2).astype(jnp.int32)
    row_total = MB * ROWS
    flattened_rows = activations.reshape(row_total, MODEL_WIDTH)
    row_pages = page_of_row.reshape(row_total)
    rows_per_block = math.gcd(row_total, 32)

    def adapter_block(packed_weights):
        rows_blk, pages_blk = packed_weights
        shrink_rows = jnp.take(shrink_pages, pages_blk, axis=0)
        low_rank = jnp.einsum("nd,nkd->nk", rows_blk.astype(jnp.float32), shrink_rows.astype(jnp.float32),
                              precision=lax.Precision.HIGHEST).astype(jnp.bfloat16)
        expand_rows = jnp.take(expand_pages, pages_blk, axis=0)
        return jnp.einsum("nk,nkf->nf", low_rank.astype(jnp.float32), expand_rows.astype(jnp.float32),
                          precision=lax.Precision.HIGHEST)

    adapter_delta = lax.map(adapter_block, (flattened_rows.reshape(-1, rows_per_block, MODEL_WIDTH),
                                  row_pages.reshape(-1, rows_per_block))).reshape(row_total, FF)
    gate_value = jnp.dot(flattened_rows, gate_matrix, preferred_element_type=jnp.float32)
    up_activation = jnp.dot(flattened_rows, up_weight, preferred_element_type=jnp.float32) + adapter_scale * adapter_delta
    hidden = (jax.nn.silu(gate_value) * up_activation).astype(jnp.bfloat16)
    layer_out = jnp.dot(hidden, down_matrix, preferred_element_type=jnp.float32).astype(jnp.bfloat16)
    return layer_out.reshape(MB, ROWS, MODEL_WIDTH)
```

```python
import functools

import jax
import jax.numpy as jnp
from jax import lax
from jax.experimental import pallas as pl
from jax.experimental.pallas import tpu as pltpu
from jax.sharding import PartitionSpec as P

MESH = pl.DeviceIdType.MESH
F32 = jnp.float32
BF16 = jnp.bfloat16
adapter_scale = 2.0

NY, NZ, NX = 8, 8, 4
NPOOL = NZ * NX


def mod(a, n):
    return lax.rem(a + n, n)


def remote(src, dst, ssem, rsem, device):
    return pltpu.make_async_remote_copy(
        src_ref=src, dst_ref=dst, send_sem=ssem, recv_sem=rsem, device_id=device, device_id_type=MESH
    )


def kernel(
    acts, gate, up, down, shrink, expand, rowad, ptab, out,
    abuf, gbuf, ubuf, dbuf, sbuf, ebuf, esel, epar, e8, blocks, wide, lrs, lrr, lr8,
    gacc, uacc, gpart, upart, grecv, urecv, hid, xs, xr, zs, zr, zg, obuf,
    lsem, psend, precv, esend, erecv, wsend, wrecv, lsend, lrecv, gsend, grsem, usend, ursem,
    hsend, hrecv, xsend, xrecv, zsend, zrecv, fsend, frecv, osend, orecv,
):
    rows, width = abuf.shape[1], abuf.shape[2]
    hidden = gbuf.shape[2]
    piece = rows // NY
    p = lax.axis_index("pool")
    t = lax.axis_index("tp")
    c = lax.rem(t, 2)
    o = 1 - c
    y = t // 2
    z = p // NX
    x = lax.rem(p, NX)
    partner = (p, 2 * y + o)

    def at_y(n):
        return (p, 2 * mod(y + n, NY) + c)

    def at_z(n):
        return (mod(z + n, NZ) * NX + x, t)

    def at_x(n):
        return (z * NX + mod(x + n, NX), t)

    bar = pltpu.get_barrier_semaphore()
    pl.semaphore_signal(bar, inc=1, device_id=partner, device_id_type=MESH)
    for n in range(1, NY):
        pl.semaphore_signal(bar, inc=1, device_id=at_y(n), device_id_type=MESH)

    def greet(n, carry):
        pl.semaphore_signal(bar, inc=1, device_id=(mod(p + n, NPOOL), t), device_id_type=MESH)
        return carry

    lax.fori_loop(1, NPOOL, greet, 0)
    for n in range(1, NX):
        pl.semaphore_signal(
            bar, inc=1, device_id=(z * NX + mod(x + n, NX), 2 * y + o), device_id_type=MESH
        )

    loads = [
        pltpu.make_async_copy(expand, ebuf, lsem.at[0]),
        pltpu.make_async_copy(acts.at[c], abuf.at[c], lsem.at[1]),
        pltpu.make_async_copy(shrink, sbuf.at[c], lsem.at[2]),
        pltpu.make_async_copy(gate, gbuf.at[c], lsem.at[3]),
        pltpu.make_async_copy(up, ubuf.at[c], lsem.at[4]),
        pltpu.make_async_copy(down, dbuf.at[c], lsem.at[5]),
    ]
    for cp in loads:
        cp.start()

    table = jnp.broadcast_to(ptab[...].astype(F32).astype(BF16), (8, ptab.shape[1]))
    base = (p * expand.shape[0]).astype(F32)
    rel = []
    for m in range(2):
        ids = jnp.broadcast_to(rowad[m : m + 1, :], (ptab.shape[1], rows))
        hot = (lax.broadcasted_iota(jnp.int32, ids.shape, 0) == ids).astype(F32).astype(BF16)
        rel.append(jnp.dot(table, hot, preferred_element_type=F32) - base)
    rel_mine = jnp.where(c == 0, rel[0], rel[1])
    rel_other = jnp.where(c == 0, rel[1], rel[0])
    pages = expand.shape[0]

    def used(r, j):
        return jnp.max(jnp.where(r == float(j), 1.0, 0.0), axis=1, keepdims=True)

    use_mine = [used(rel_mine, j) for j in range(pages)]
    use_other = [used(rel_other, j) for j in range(pages)]
    row_mask = (rel_mine[0:1, :] > -0.5) & (rel_mine[0:1, :] < pages - 0.5)

    loads[0].wait()
    chunk = 2048

    def pick(i, carry):
        cols = pl.ds(pl.multiple_of(i * chunk, chunk), chunk)
        mine = jnp.zeros((ebuf.shape[1], chunk), F32)
        other = jnp.zeros((ebuf.shape[1], chunk), F32)
        for j in range(pages):
            page = ebuf[j, :, cols].astype(F32)
            mine = mine + page * use_mine[j][:4]
            other = other + page * use_other[j][:4]
        esel[0, :, cols] = mine.astype(BF16)
        esel[1, :, cols] = other.astype(BF16)
        return carry

    lax.fori_loop(0, ebuf.shape[2] // chunk, pick, 0)

    for cp in loads[1:]:
        cp.wait()
    pl.semaphore_wait(bar, 1 + (NY - 1) + (NPOOL - 1) + (NX - 1))

    ex = [
        remote(esel.at[1], epar, psend.at[0], precv.at[0], partner),
        remote(acts.at[o], abuf.at[c], psend.at[1], precv.at[1], partner),
        remote(sbuf.at[c], sbuf.at[c], psend.at[2], precv.at[2], partner),
        remote(gbuf.at[c], gbuf.at[c], psend.at[3], precv.at[3], partner),
        remote(ubuf.at[c], ubuf.at[c], psend.at[4], precv.at[4], partner),
        remote(dbuf.at[c], dbuf.at[c], psend.at[5], precv.at[5], partner),
    ]
    for cp in ex:
        cp.start()

    gacc[...] = jnp.dot(abuf[c], gbuf[c], preferred_element_type=F32)
    uacc[...] = jnp.dot(abuf[c], ubuf[c], preferred_element_type=F32)

    ex[0].wait_recv()

    def join(i, carry):
        cols = pl.ds(pl.multiple_of(i * chunk, chunk), chunk)
        a = esel[0, :, cols].astype(F32)
        b = epar[:, cols].astype(F32)
        low = jnp.where(c == 0, a, b)
        high = jnp.where(c == 0, b, a)
        e8[:, cols] = jnp.concatenate([low, high], axis=0).astype(BF16)
        return carry

    lax.fori_loop(0, ebuf.shape[2] // chunk, join, 0)

    def block_to(n):
        q = mod(p + n, NPOOL)
        return remote(
            e8.at[:, pl.ds(pl.multiple_of(q * hidden, 128), hidden)],
            blocks.at[p],
            esend.at[n],
            erecv.at[p],
            (q, t),
        )

    def send_block(n, carry):
        block_to(n).start()
        return carry

    lax.fori_loop(1, NPOOL, send_block, 0)
    blocks[p] = e8[:, pl.ds(pl.multiple_of(p * hidden, 128), hidden)]

    ex[1].wait_recv()
    ex[2].wait_recv()
    low = jnp.zeros((sbuf.shape[2], rows), F32)
    for half in range(2):
        factor = jnp.zeros(sbuf.shape[2:], F32)
        for j in range(pages):
            factor = factor + sbuf[half, j].astype(F32) * use_mine[j][0:1]
        low = low + lax.dot_general(
            factor.astype(BF16), abuf[half], (((1,), (1,)), ((), ())), preferred_element_type=F32
        )
    low = jnp.where(row_mask, low, 0.0)
    for k in range(NY):
        lrs[k] = low[8 * k : 8 * k + 8, :]
    lcopy = []
    for n in range(1, NY):
        cp = remote(lrs.at[mod(y + n, NY)], lrr.at[n], lsend.at[n], lrecv.at[n], at_y(n))
        cp.start()
        lcopy.append(cp)

    ex[3].wait_recv()
    gacc[...] += jnp.dot(abuf[o], gbuf[o], preferred_element_type=F32)
    gpart[...] = gacc[...].astype(BF16).reshape(gpart.shape)
    gcopy = []
    for n in (4, 3, 5, 2, 6, 1, 7):
        cp = remote(gpart.at[mod(y + n, NY)], grecv.at[n], gsend.at[n], grsem.at[n], at_y(n))
        cp.start()
        gcopy.append(cp)

    total = lrs[y]
    for n in range(1, NY):
        lcopy[n - 1].wait_recv()
        total = total + lrr[n]
    lr8[...] = total.astype(BF16)

    def rank_to(n):
        q = mod(p + n, NPOOL)
        return remote(lr8, wide.at[p], wsend.at[n], wrecv.at[p], (q, t))

    def send_rank(n, carry):
        rank_to(n).start()
        return carry

    lax.fori_loop(1, NPOOL, send_rank, 0)
    wide[p] = lr8[...]

    ex[4].wait_recv()
    uacc[...] += jnp.dot(abuf[o], ubuf[o], preferred_element_type=F32)

    def arrived(n, carry):
        q = mod(p + n, NPOOL)
        remote(e8.at[:, pl.ds(0, hidden)], blocks.at[q], esend.at[n], erecv.at[q], (q, t)).wait_recv()
        remote(lr8, wide.at[q], wsend.at[n], wrecv.at[q], (q, t)).wait_recv()
        return carry

    lax.fori_loop(1, NPOOL, arrived, 0)
    wide_all = wide[...].reshape(NPOOL * 8, rows)
    block_all = blocks[...].reshape(NPOOL * 8, hidden)
    uacc[...] += adapter_scale * lax.dot_general(
        wide_all, block_all, (((0,), (0,)), ((), ())), preferred_element_type=F32
    )
    upart[...] = uacc[...].astype(BF16).reshape(upart.shape)
    ucopy = []
    for n in (4, 3, 5, 2, 6, 1, 7):
        cp = remote(upart.at[mod(y + n, NY)], urecv.at[n], usend.at[n], ursem.at[n], at_y(n))
        cp.start()
        ucopy.append(cp)

    mine = pl.ds(pl.multiple_of(y * piece, piece), piece)
    g = gacc[mine, :]
    for n in (7, 1, 6, 2, 5, 3, 4):
        remote(gpart.at[0], grecv.at[n], gsend.at[n], grsem.at[n], at_y(n)).wait_recv()
        g = g + grecv[n].astype(F32)
    act = g / (1.0 + jnp.exp(-g))
    u = uacc[mine, :]
    for n in (7, 1, 6, 2, 5, 3, 4):
        remote(upart.at[0], urecv.at[n], usend.at[n], ursem.at[n], at_y(n)).wait_recv()
        u = u + urecv[n].astype(F32)
    hid[0] = (act * u).astype(BF16)
    hcopy = []
    for n in (4, 3, 5, 2, 6, 1, 7):
        cp = remote(hid.at[0], hid.at[n], hsend.at[n], hrecv.at[n], at_y(n))
        cp.start()
        hcopy.append(cp)

    ex[5].wait_recv()
    order = (0, 7, 1, 6, 2, 5, 3, 4)
    cols = xs.shape[3]

    def down_piece(n):
        h = hid[n]
        for half in range(2):
            part = jnp.dot(h, dbuf[half], preferred_element_type=F32).astype(BF16)
            xs[n, 2 * half] = part[:, :cols]
            xs[n, 2 * half + 1] = part[:, cols:]
        for k in (2, 1, 3):
            remote(
                xs.at[n, mod(x + k, NX)], xr.at[n, k], xsend.at[n, k], xrecv.at[n, k], at_x(k)
            ).start()

    def x_done(n):
        total = xs[n, x].astype(F32)
        for k in (1, 2, 3):
            remote(xs.at[n, 0], xr.at[n, k], xsend.at[n, k], xrecv.at[n, k], at_x(k)).wait_recv()
            total = total + xr[n, k].astype(F32)
        zs[n] = total.astype(BF16)
        owner = mod(y - n + NY, NY)

        @pl.when(owner == z)
        def _():
            zr[z] = zs[n]

        @pl.when(owner != z)
        def _():
            remote(
                zs.at[n], zr.at[z], zsend.at[n], zrecv.at[z], (owner * NX + x, t)
            ).start()

    for i, n in enumerate(order):
        if n > 0:
            remote(hid.at[0], hid.at[n], hsend.at[n], hrecv.at[n], at_y(n)).wait_recv()
        down_piece(n)
        if i > 1:
            x_done(order[i - 2])
    x_done(order[-2])
    x_done(order[-1])

    total = zr[z].astype(F32)
    for k in range(1, NZ):
        q = mod(z + k, NZ)
        remote(zs.at[0], zr.at[q], zsend.at[0], zrecv.at[q], at_z(k)).wait_recv()
        total = total + zr[q].astype(F32)
    here = pl.ds(pl.multiple_of(z * piece, piece), piece)
    zg[here, :] = total.astype(BF16)
    for k in (4, 3, 5, 2, 6, 1, 7):
        remote(zg.at[here], zg.at[here], fsend.at[k], frecv.at[k], at_z(k)).start()
    for k in range(1, NZ):
        there = pl.ds(pl.multiple_of(mod(z - k + NZ, NZ) * piece, piece), piece)
        remote(zg.at[here], zg.at[there], fsend.at[k], frecv.at[k], at_z(k)).wait_recv()

    side = x // 2
    odd = lax.rem(x, 2)
    place = obuf.at[c, :, pl.ds(pl.multiple_of(odd * cols, cols), cols)]
    for k in (2, 1, 3):
        remote(
            zg, place, osend.at[k], orecv.at[odd, c], (z * NX + mod(x + k, NX), 2 * y + side)
        ).start()

    @pl.when(side != c)
    def _():
        remote(zg, place, osend.at[0], orecv.at[odd, c], partner).start()

    @pl.when(side == c)
    def _():
        obuf[c, :, pl.ds(pl.multiple_of(odd * cols, cols), cols)] = zg[...]

    for a in range(2):
        for m in range(2):

            @pl.when(jnp.logical_or(2 * c + a != x, m != c))
            def _():
                remote(
                    zg, obuf.at[m, :, a * cols : (a + 1) * cols], osend.at[0], orecv.at[a, m], partner
                ).wait_recv()

    final = pltpu.make_async_copy(obuf, out, lsem.at[6])
    final.start()

    for cp in ex:
        cp.wait_send()
    for cp in lcopy + gcopy + ucopy + hcopy:
        cp.wait_send()

    def left(n, carry):
        block_to(n).wait_send()
        rank_to(n).wait_send()
        return carry

    lax.fori_loop(1, NPOOL, left, 0)
    for n in range(NY):
        for k in range(1, NX):
            remote(xs.at[n, 0], xr.at[n, k], xsend.at[n, k], xrecv.at[n, k], at_x(k)).wait_send()

        @pl.when(mod(y - n + NY, NY) != z)
        def _():
            remote(zs.at[n], zr.at[0], zsend.at[n], zrecv.at[0], at_z(1)).wait_send()

    for k in range(1, NZ):
        remote(zg.at[here], zg.at[here], fsend.at[k], frecv.at[k], at_z(k)).wait_send()
    for k in range(1, NX):
        remote(zg, place, osend.at[k], orecv.at[odd, c], partner).wait_send()

    @pl.when(side != c)
    def _():
        remote(zg, place, osend.at[0], orecv.at[odd, c], partner).wait_send()

    final.wait()


def on_device(acts, gate, up, down, shrink, expand, row_adapter, page_table):
    batches, rows, width = acts.shape
    hidden = gate.shape[1]
    out_width = down.shape[1]
    pages, rank, _ = shrink.shape
    rank_local, ff = expand.shape[1:]
    piece = rows // NY
    cols = 2 * out_width // NX
    anyspec = pl.BlockSpec(memory_space=pl.ANY)
    vmem = pl.BlockSpec(memory_space=pltpu.VMEM)
    dma = pltpu.SemaphoreType.DMA
    scratch = [
        pltpu.VMEM((2, rows, width), BF16),
        pltpu.VMEM((2, width, hidden), BF16),
        pltpu.VMEM((2, width, hidden), BF16),
        pltpu.VMEM((2, hidden, out_width), BF16),
        pltpu.VMEM((2, pages, rank, width), BF16),
        pltpu.VMEM((pages, rank_local, ff), BF16),
        pltpu.VMEM((2, rank_local, ff), BF16),
        pltpu.VMEM((rank_local, ff), BF16),
        pltpu.VMEM((2 * rank_local, ff), BF16),
        pltpu.VMEM((NPOOL, 2 * rank_local, hidden), BF16),
        pltpu.VMEM((NPOOL, 2 * rank_local, rows), BF16),
        pltpu.VMEM((NY, 2 * rank_local, rows), F32),
        pltpu.VMEM((NY, 2 * rank_local, rows), F32),
        pltpu.VMEM((2 * rank_local, rows), BF16),
        pltpu.VMEM((rows, hidden), F32),
        pltpu.VMEM((rows, hidden), F32),
        pltpu.VMEM((NY, piece, hidden), BF16),
        pltpu.VMEM((NY, piece, hidden), BF16),
        pltpu.VMEM((NY, piece, hidden), BF16),
        pltpu.VMEM((NY, piece, hidden), BF16),
        pltpu.VMEM((NY, piece, hidden), BF16),
        pltpu.VMEM((NY, NX, piece, cols), BF16),
        pltpu.VMEM((NY, NX, piece, cols), BF16),
        pltpu.VMEM((NY, piece, cols), BF16),
        pltpu.VMEM((NZ, piece, cols), BF16),
        pltpu.VMEM((rows, cols), BF16),
        pltpu.VMEM((batches, rows, out_width), BF16),
        dma((8,)),
        dma((6,)), dma((6,)),
        dma((NPOOL,)), dma((NPOOL,)),
        dma((NPOOL,)), dma((NPOOL,)),
        dma((NY,)), dma((NY,)),
        dma((NY,)), dma((NY,)),
        dma((NY,)), dma((NY,)),
        dma((NY,)), dma((NY,)),
        dma((NY, NX)), dma((NY, NX)),
        dma((NY,)), dma((NZ,)),
        dma((NZ,)), dma((NZ,)),
        dma((NX,)), dma((2, 2)),
    ]
    return pl.pallas_call(
        kernel,
        out_shape=jax.ShapeDtypeStruct((batches, rows, out_width), BF16),
        in_specs=[anyspec] * 6 + [vmem] * 2,
        out_specs=anyspec,
        scratch_shapes=scratch,
        compiler_params=pltpu.CompilerParams(
            collective_id=0, has_side_effects=True, vmem_limit_bytes=56 * 2**20
        ),
        name="layer",
    )(acts, gate, up, down, shrink, expand, row_adapter, page_table.reshape(1, -1))


def solution(mesh):
    return jax.shard_map(
        on_device,
        mesh=mesh,
        in_specs=(
            P(None, None, "tp"),
            P("tp", "pool"),
            P("tp", "pool"),
            P("pool", "tp"),
            P("pool", None, "tp"),
            P("pool", "tp", None),
            P(),
            P(),
        ),
        out_specs=P(None, None, "tp"),
        check_vma=False,
    )
```

```python
import functools

import jax
import jax.numpy as jnp
from jax import lax
from jax.experimental import pallas as pl
from jax.experimental.pallas import tpu as pltpu
from jax.sharding import PartitionSpec as P

MESH = pl.DeviceIdType.MESH
F32 = jnp.float32
BF16 = jnp.bfloat16
adapter_scale = 2.0

NY, NZ, NX = 8, 8, 4
NPOOL = NZ * NX
FIRST, LAST = 6, 26
VMEM_LIMIT = 24 * 2**20


def mod(a, n):
    return lax.rem(a + n, n)


def remote(src, dst, ssem, rsem, device):
    return pltpu.make_async_remote_copy(
        src_ref=src, dst_ref=dst, send_sem=ssem, recv_sem=rsem, device_id=device, device_id_type=MESH
    )


def kernel(
    acts, gate, up, down, shrink, expand, row_ids, pages_at, out, rowad, ptab,
    aloc, apar, gown, gpar, uown, upar, dbuf, sbuf, ebuf, esel, epar, e8, blocks, wide,
    lroth, lrpar, lrs, lrr, lr8, lrx, lrz, gacc, uacc, gpart, upart, act,
    m4, m2, f3, f1, hid, xs, xr, zs, zr, zg, obuf,
    lsem, psend, precv, esend, erecv, lsend, lrecv, lxs, lxr, lzs, lzr, rsend, rrecv,
    hsend, hrecv, xsend, xrecv, zsend, zrecv, fsend, frecv, osend, orecv,
):
    rows = apar.shape[0]
    hidden = gown.shape[1]
    pages = expand.shape[0]
    piece = rows // NY
    part_rows = piece // 2
    half_rows = part_rows // 2
    p = lax.axis_index("pool")
    t = lax.axis_index("tp")
    c = lax.rem(t, 2)
    o = 1 - c
    y = t // 2
    z = p // NX
    x = lax.rem(p, NX)
    partner = (p, 2 * y + o)
    pending = []

    def go(src, dst, ssem, rsem, device):
        cp = remote(src, dst, ssem, rsem, device)
        cp.start()
        pending.append(cp)

    def come(src, dst, ssem, rsem):
        remote(src, dst, ssem, rsem, partner).wait_recv()

    def at_y(n):
        return (p, 2 * mod(y + n + NY, NY) + c)

    def at_z(n):
        return (mod(z + n, NZ) * NX + x, t)

    def at_x(n):
        return (z * NX + mod(x + n, NX), t)

    bar = pltpu.get_barrier_semaphore()

    def greet(n, carry):
        pl.semaphore_signal(bar, inc=1, device_id=(mod(p + n, NPOOL), t), device_id_type=MESH)
        return carry

    lax.fori_loop(1, NPOOL, greet, 0)
    for n in (4, 3, 5, 2, 6, 1, 7):
        pl.semaphore_signal(bar, inc=1, device_id=at_y(n), device_id_type=MESH)
    for n in range(1, NX):
        pl.semaphore_signal(
            bar, inc=1, device_id=(z * NX + mod(x + n, NX), 2 * y + o), device_id_type=MESH
        )
    pl.semaphore_signal(bar, inc=1, device_id=partner, device_id_type=MESH)

    loads = [
        pltpu.make_async_copy(shrink, sbuf, lsem.at[0]),
        pltpu.make_async_copy(acts, aloc, lsem.at[1]),
        pltpu.make_async_copy(expand, ebuf, lsem.at[2]),
        pltpu.make_async_copy(gate, gown, lsem.at[3]),
        pltpu.make_async_copy(up, uown, lsem.at[4]),
        pltpu.make_async_copy(down, dbuf.at[c], lsem.at[5]),
    ]
    small = [
        pltpu.make_async_copy(row_ids, rowad, lsem.at[6]),
        pltpu.make_async_copy(pages_at, ptab, lsem.at[7]),
    ]
    for cp in small:
        cp.start()
    for cp in loads:
        cp.start()

    for cp in small:
        cp.wait()
    table = jnp.broadcast_to(ptab[...].astype(F32).astype(BF16), (8, ptab.shape[1]))
    base = (p * pages).astype(F32)
    rel = []
    for m in range(2):
        ids = jnp.broadcast_to(rowad[m : m + 1, :], (ptab.shape[1], rows))
        hot = (lax.broadcasted_iota(jnp.int32, ids.shape, 0) == ids).astype(F32).astype(BF16)
        rel.append(jnp.dot(table, hot, preferred_element_type=F32) - base)
    rel_mine = jnp.where(c == 0, rel[0], rel[1])
    rel_other = jnp.where(c == 0, rel[1], rel[0])

    def used(r, j):
        return jnp.max(jnp.where(r == float(j), 1.0, 0.0), axis=1, keepdims=True)

    use_mine = [used(rel_mine, j) for j in range(pages)]
    use_other = [used(rel_other, j) for j in range(pages)]
    row_mask = (rel_mine[0:1, :] > -0.5) & (rel_mine[0:1, :] < pages - 0.5)

    loads[0].wait()
    loads[1].wait()

    def low_part(use, a):
        factor = jnp.zeros(sbuf.shape[1:], F32)
        for j in range(pages):
            factor = factor + sbuf[j].astype(F32) * use[j][0:1]
        return lax.dot_general(
            factor.astype(BF16), a, (((1,), (1,)), ((), ())), preferred_element_type=F32
        )

    low = low_part(use_mine, aloc[c])
    lroth[...] = low_part(use_other, aloc[o])

    loads[2].wait()
    chunk = 2048

    def pick(i, carry):
        cols = pl.ds(pl.multiple_of(i * chunk, chunk), chunk)
        mine = jnp.zeros((ebuf.shape[1], chunk), F32)
        other = jnp.zeros((ebuf.shape[1], chunk), F32)
        for j in range(pages):
            page = ebuf[j, :, cols].astype(F32)
            mine = mine + page * use_mine[j][:4]
            other = other + page * use_other[j][:4]
        esel[0, :, cols] = mine.astype(BF16)
        esel[1, :, cols] = other.astype(BF16)
        return carry

    lax.fori_loop(0, ebuf.shape[2] // chunk, pick, 0)

    for cp in loads[3:]:
        cp.wait()
    gacc[...] = jnp.dot(aloc[c], gown[...], preferred_element_type=F32)
    uacc[...] = jnp.dot(aloc[c], uown[...], preferred_element_type=F32)
    pl.semaphore_wait(bar, 1 + (NY - 1) + (NPOOL - 1) + (NX - 1))

    ex = [
        remote(lroth, lrpar, psend.at[0], precv.at[0], partner),
        remote(esel.at[1], epar, psend.at[1], precv.at[1], partner),
        remote(aloc.at[o], apar, psend.at[2], precv.at[2], partner),
        remote(gown, gpar, psend.at[3], precv.at[3], partner),
        remote(uown, upar, psend.at[4], precv.at[4], partner),
        remote(dbuf.at[c], dbuf.at[c], psend.at[5], precv.at[5], partner),
    ]
    for cp in ex:
        cp.start()

    ex[0].wait_recv()
    low = jnp.where(row_mask, low + lrpar[...], 0.0)
    for k in range(NY):
        lrs[k] = low[8 * k : 8 * k + 8, :]
    for n in (4, 3, 5, 2, 6, 1, 7):
        go(lrs.at[mod(y + n, NY)], lrr.at[n], lsend.at[n], lrecv.at[n], at_y(n))

    ex[1].wait_recv()

    def join(i, carry):
        cols = pl.ds(pl.multiple_of(i * chunk, chunk), chunk)
        a = esel[0, :, cols].astype(F32)
        b = epar[:, cols].astype(F32)
        e8[:, cols] = jnp.concatenate(
            [jnp.where(c == 0, a, b), jnp.where(c == 0, b, a)], axis=0
        ).astype(BF16)
        return carry

    lax.fori_loop(0, ebuf.shape[2] // chunk, join, 0)

    def block_to(n):
        q = mod(p + n, NPOOL)
        return remote(
            e8.at[:, pl.ds(pl.multiple_of(q * hidden, 128), hidden)],
            blocks.at[p],
            esend.at[n],
            erecv.at[p],
            (q, t),
        )

    def send_block(n, carry):
        block_to(n).start()
        return carry

    lax.fori_loop(FIRST, LAST, send_block, 0)
    blocks[p] = e8[:, pl.ds(pl.multiple_of(p * hidden, 128), hidden)]

    def own_rows(dest, first, count):
        return pl.ds(pl.multiple_of(dest * piece + first, 8), count)

    def spans(s, h):
        near = h * part_rows + s * half_rows
        far = h * part_rows + (1 - s) * half_rows
        return near, far

    def sum_first(q, part, h):
        for s in range(2):
            d = 1 - 2 * s
            near, far = spans(s, h)
            go(
                part.at[mod(y + 4, NY), near : near + half_rows],
                m4.at[q, s, h],
                rsend.at[q, 0, s, h],
                rrecv.at[q, 0, s, h],
                at_y(d),
            )
            go(
                part.at[mod(y + 2 * d + NY, NY), h * part_rows : (h + 1) * part_rows],
                m2.at[q, s, h],
                rsend.at[q, 1, s, h],
                rrecv.at[q, 1, s, h],
                at_y(d),
            )
        for s in range(2):
            d = 1 - 2 * s
            near, far = spans(s, h)
            go(
                part.at[mod(y + 3 * d + NY, NY), far : far + half_rows],
                f3.at[q, s, far : far + half_rows],
                rsend.at[q, 2, s, h],
                rrecv.at[q, 2, s, h],
                at_y(3 * d),
            )

    def sum_second(q, part, acc, h):
        for s in range(2):
            d = 1 - 2 * s
            near, far = spans(s, h)
            dest = mod(y + 3 * d + NY, NY)
            come(m4.at[q, s, h], m4.at[q, s, h], rsend.at[q, 0, s, h], rrecv.at[q, 0, s, h])
            part[dest, near : near + half_rows, :] = (
                acc[own_rows(dest, near, half_rows), :] + m4[q, s, h].astype(F32)
            ).astype(BF16)
            go(
                part.at[dest, near : near + half_rows],
                f3.at[q, s, near : near + half_rows],
                rsend.at[q, 3, s, h],
                rrecv.at[q, 3, s, h],
                at_y(3 * d),
            )
        for s in range(2):
            d = 1 - 2 * s
            dest = mod(y + d + NY, NY)
            come(m2.at[q, s, h], m2.at[q, s, h], rsend.at[q, 1, s, h], rrecv.at[q, 1, s, h])
            part[dest, h * part_rows : (h + 1) * part_rows, :] = (
                acc[own_rows(dest, h * part_rows, part_rows), :] + m2[q, s, h].astype(F32)
            ).astype(BF16)
            go(
                part.at[dest, h * part_rows : (h + 1) * part_rows],
                f1.at[q, s, h],
                rsend.at[q, 4, s, h],
                rrecv.at[q, 4, s, h],
                at_y(d),
            )

    def sum_last(q, acc, h):
        total = acc[own_rows(y, h * part_rows, part_rows), :]
        span = slice(h * part_rows, (h + 1) * part_rows)
        for s in range(2):
            near, far = spans(s, h)
            a = f3.at[q, s, far : far + half_rows]
            b = f3.at[q, s, near : near + half_rows]
            come(a, a, rsend.at[q, 2, s, h], rrecv.at[q, 2, s, h])
            come(b, b, rsend.at[q, 3, s, h], rrecv.at[q, 3, s, h])
            come(f1.at[q, s, h], f1.at[q, s, h], rsend.at[q, 4, s, h], rrecv.at[q, 4, s, h])
            total = total + f3[q, s, span, :].astype(F32) + f1[q, s, h].astype(F32)
        return total

    ex[2].wait_recv()
    ex[3].wait_recv()
    gacc[...] += jnp.dot(apar[...], gpar[...], preferred_element_type=F32)
    gpart[...] = gacc[...].astype(BF16).reshape(gpart.shape)
    for h in range(2):
        sum_first(0, gpart, h)

    total = lrs[y]
    for n in range(1, NY):
        come(lrs.at[0], lrr.at[n], lsend.at[n], lrecv.at[n])
        total = total + lrr[n]
    lr8[0] = total.astype(BF16)
    for k in (2, 1, 3):
        go(lr8.at[0], lrx.at[k], lxs.at[k], lxr.at[k], at_x(k))

    for h in range(2):
        sum_second(0, gpart, gacc, h)

    total = lr8[0].astype(F32)
    for k in range(1, NX):
        come(lr8.at[0], lrx.at[k], lxs.at[k], lxr.at[k])
        total = total + lrx[k].astype(F32)
    lr8[1] = total.astype(BF16)
    for k in (4, 3, 5, 2, 6, 1, 7):
        go(lr8.at[1], lrz.at[k], lzs.at[k], lzr.at[k], at_z(k))
    lax.fori_loop(1, FIRST, send_block, 0)
    lax.fori_loop(LAST, NPOOL, send_block, 0)

    ex[4].wait_recv()
    uacc[...] += jnp.dot(apar[...], upar[...], preferred_element_type=F32)

    total = lr8[1].astype(F32)
    for k in range(1, NZ):
        come(lr8.at[1], lrz.at[k], lzs.at[k], lzr.at[k])
        total = total + lrz[k].astype(F32)
    page = rel_mine + base
    for q in range(NPOOL):
        owned = (page > q * pages - 0.5) & (page < (q + 1) * pages - 0.5)
        wide[q] = jnp.where(owned, total, 0.0).astype(BF16)

    for h in range(2):
        g = sum_last(0, gacc, h)
        act[h * part_rows : (h + 1) * part_rows, :] = g / (1.0 + jnp.exp(-g))

    def arrived(n, carry):
        q = mod(p + n, NPOOL)
        remote(e8.at[:, pl.ds(0, hidden)], blocks.at[q], esend.at[n], erecv.at[q], (q, t)).wait_recv()
        return carry

    lax.fori_loop(1, NPOOL, arrived, 0)
    wide_all = wide[...].reshape(NPOOL * 8, rows)
    block_all = blocks[...].reshape(NPOOL * 8, hidden)
    uacc[...] += adapter_scale * lax.dot_general(
        wide_all, block_all, (((0,), (0,)), ((), ())), preferred_element_type=F32
    )
    upart[...] = uacc[...].astype(BF16).reshape(upart.shape)
    for h in range(2):
        sum_first(1, upart, h)
    for h in range(2):
        sum_second(1, upart, uacc, h)

    def share_first(h):
        span = slice(h * part_rows, (h + 1) * part_rows)
        hid[0, span, :] = (act[span, :] * sum_last(1, uacc, h)).astype(BF16)
        for s in range(2):
            d = 1 - 2 * s
            one, three = (1, 3) if s == 0 else (7, 5)
            go(
                hid.at[0, span], hid.at[one, span],
                hsend.at[0, s, h], hrecv.at[0, s, h], at_y(d),
            )
            go(
                hid.at[0, span], hid.at[three, span],
                hsend.at[1, s, h], hrecv.at[1, s, h], at_y(3 * d),
            )

    def share_second(h):
        span = slice(h * part_rows, (h + 1) * part_rows)
        for s in range(2):
            d = 1 - 2 * s
            one, two = (1, 2) if s == 0 else (7, 6)
            come(hid.at[one, span], hid.at[one, span], hsend.at[0, s, h], hrecv.at[0, s, h])
            go(
                hid.at[one, span], hid.at[two, span],
                hsend.at[2, s, h], hrecv.at[2, s, h], at_y(d),
            )
        for s in range(2):
            d = 1 - 2 * s
            three = 3 if s == 0 else 5
            near, far = spans(s, h)
            come(hid.at[three, span], hid.at[three, span], hsend.at[1, s, h], hrecv.at[1, s, h])
            go(
                hid.at[three, near : near + half_rows], hid.at[4, near : near + half_rows],
                hsend.at[3, s, h], hrecv.at[3, s, h], at_y(d),
            )

    def shared(n):
        for h in range(2):
            span = slice(h * part_rows, (h + 1) * part_rows)
            if n in (2, 6):
                s = 0 if n == 2 else 1
                come(hid.at[n, span], hid.at[n, span], hsend.at[2, s, h], hrecv.at[2, s, h])
            if n == 4:
                for s in range(2):
                    near, far = spans(s, h)
                    v = hid.at[4, near : near + half_rows]
                    come(v, v, hsend.at[3, s, h], hrecv.at[3, s, h])

    for h in range(2):
        share_first(h)

    ex[5].wait_recv()
    cols = xs.shape[3]

    def down_piece(n):
        shared(n)
        for half in range(2):
            part = jnp.dot(hid[n], dbuf[half], preferred_element_type=F32).astype(BF16)
            xs[n, 2 * half] = part[:, :cols]
            xs[n, 2 * half + 1] = part[:, cols:]
        for k in (2, 1, 3):
            go(xs.at[n, mod(x + k, NX)], xr.at[n, k], xsend.at[n, k], xrecv.at[n, k], at_x(k))

    def x_done(n):
        total = xs[n, x].astype(F32)
        for k in (1, 2, 3):
            come(xs.at[n, 0], xr.at[n, k], xsend.at[n, k], xrecv.at[n, k])
            total = total + xr[n, k].astype(F32)
        zs[n] = total.astype(BF16)
        owner = mod(y - n + NY, NY)

        @pl.when(owner == z)
        def _():
            zr[z] = zs[n]

        @pl.when(owner != z)
        def _():
            remote(zs.at[n], zr.at[z], zsend.at[n], zrecv.at[z], (owner * NX + x, t)).start()

    down_piece(0)
    for h in range(2):
        share_second(h)
    order = (0, 1, 7, 3, 5, 2, 6, 4)
    for i, n in enumerate(order):
        if n > 0:
            down_piece(n)
        if i > 1:
            x_done(order[i - 2])
    x_done(order[-2])
    x_done(order[-1])

    total = zr[z].astype(F32)
    for k in range(1, NZ):
        q = mod(z + k, NZ)
        come(zs.at[0], zr.at[q], zsend.at[0], zrecv.at[q])
        total = total + zr[q].astype(F32)

    def block_rows(k):
        return pl.ds(pl.multiple_of(mod(z - k + NZ, NZ) * piece, piece), piece)

    here = block_rows(0)
    zg[here, :] = total.astype(BF16)
    for k in (4, 3, 5, 2, 6, 1, 7):
        go(zg.at[here], zg.at[here], fsend.at[k], frecv.at[k], at_z(k))

    side = x // 2
    odd = lax.rem(x, 2)
    place = pl.ds(pl.multiple_of(odd * cols, cols), cols)
    for k in (0, 1, 7, 2, 6, 3, 5, 4):
        there = block_rows(k)
        if k > 0:
            come(zg.at[here], zg.at[there], fsend.at[k], frecv.at[k])
        slot = mod(z - k + NZ, NZ)
        for n in (2, 1, 3):
            go(
                zg.at[there],
                obuf.at[c, there, place],
                osend.at[k, n],
                orecv.at[odd, c, slot],
                (z * NX + mod(x + n, NX), 2 * y + side),
            )

        @pl.when(side != c)
        def _():
            remote(
                zg.at[there], obuf.at[c, there, place], osend.at[k, 0], orecv.at[odd, c, slot], partner
            ).start()

        @pl.when(side == c)
        def _():
            obuf[c, there, place] = zg[there, :]

    for a in range(2):
        for m in range(2):

            @pl.when(jnp.logical_or(2 * c + a != x, m != c))
            def _():
                for k in range(NZ):
                    v = obuf.at[m, k * piece : (k + 1) * piece, a * cols : (a + 1) * cols]
                    come(v, v, osend.at[0, 0], orecv.at[a, m, k])

    final = pltpu.make_async_copy(obuf, out, lsem.at[8])
    final.start()

    for cp in ex + pending:
        cp.wait_send()

    def left(n, carry):
        block_to(n).wait_send()
        return carry

    lax.fori_loop(1, NPOOL, left, 0)
    for n in range(NY):

        @pl.when(mod(y - n + NY, NY) != z)
        def _():
            remote(zs.at[n], zr.at[0], zsend.at[n], zrecv.at[0], at_z(1)).wait_send()

    @pl.when(side != c)
    def _():
        for k in range(NZ):
            remote(
                zg.at[here], obuf.at[c, here, place], osend.at[k, 0], orecv.at[0, 0, 0], partner
            ).wait_send()

    final.wait()


def on_device(acts, gate, up, down, shrink, expand, row_adapter, page_table):
    batches, rows, width = acts.shape
    hidden = gate.shape[1]
    out_width = down.shape[1]
    pages, rank, _ = shrink.shape
    rank_local, ff = expand.shape[1:]
    piece = rows // NY
    cols = 2 * out_width // NX
    anyspec = pl.BlockSpec(memory_space=pl.ANY)
    dma = pltpu.SemaphoreType.DMA
    ranks = 2 * rank_local
    scratch = [
        pltpu.VMEM(row_adapter.shape, jnp.int32),
        pltpu.VMEM((1, page_table.shape[0]), jnp.int32),
        pltpu.VMEM((2, rows, width), BF16),
        pltpu.VMEM((rows, width), BF16),
        pltpu.VMEM((width, hidden), BF16),
        pltpu.VMEM((width, hidden), BF16),
        pltpu.VMEM((width, hidden), BF16),
        pltpu.VMEM((width, hidden), BF16),
        pltpu.VMEM((2, hidden, out_width), BF16),
        pltpu.VMEM((pages, rank, width), BF16),
        pltpu.VMEM((pages, rank_local, ff), BF16),
        pltpu.VMEM((2, rank_local, ff), BF16),
        pltpu.VMEM((rank_local, ff), BF16),
        pltpu.VMEM((ranks, ff), BF16),
        pltpu.VMEM((NPOOL, ranks, hidden), BF16),
        pltpu.VMEM((NPOOL, ranks, rows), BF16),
        pltpu.VMEM((rank, rows), F32),
        pltpu.VMEM((rank, rows), F32),
        pltpu.VMEM((NY, ranks, rows), F32),
        pltpu.VMEM((NY, ranks, rows), F32),
        pltpu.VMEM((2, ranks, rows), BF16),
        pltpu.VMEM((NX, ranks, rows), BF16),
        pltpu.VMEM((NZ, ranks, rows), BF16),
        pltpu.VMEM((rows, hidden), F32),
        pltpu.VMEM((rows, hidden), F32),
        pltpu.VMEM((NY, piece, hidden), BF16),
        pltpu.VMEM((NY, piece, hidden), BF16),
        pltpu.VMEM((piece, hidden), F32),
        pltpu.VMEM((2, 2, 2, piece // 4, hidden), BF16),
        pltpu.VMEM((2, 2, 2, piece // 2, hidden), BF16),
        pltpu.VMEM((2, 2, piece, hidden), BF16),
        pltpu.VMEM((2, 2, 2, piece // 2, hidden), BF16),
        pltpu.VMEM((NY, piece, hidden), BF16),
        pltpu.VMEM((NY, NX, piece, cols), BF16),
        pltpu.VMEM((NY, NX, piece, cols), BF16),
        pltpu.VMEM((NY, piece, cols), BF16),
        pltpu.VMEM((NZ, piece, cols), BF16),
        pltpu.VMEM((rows, cols), BF16),
        pltpu.VMEM((batches, rows, out_width), BF16),
        dma((9,)),
        dma((6,)), dma((6,)),
        dma((NPOOL,)), dma((NPOOL,)),
        dma((NY,)), dma((NY,)),
        dma((NX,)), dma((NX,)),
        dma((NZ,)), dma((NZ,)),
        dma((2, 5, 2, 2)), dma((2, 5, 2, 2)),
        dma((4, 2, 2)), dma((4, 2, 2)),
        dma((NY, NX)), dma((NY, NX)),
        dma((NY,)), dma((NZ,)),
        dma((NZ,)), dma((NZ,)),
        dma((NZ, NX)), dma((2, 2, NZ)),
    ]
    return pl.pallas_call(
        kernel,
        out_shape=jax.ShapeDtypeStruct((batches, rows, out_width), BF16),
        in_specs=[anyspec] * 8,
        out_specs=anyspec,
        scratch_shapes=scratch,
        compiler_params=pltpu.CompilerParams(
            collective_id=0, has_side_effects=True, vmem_limit_bytes=VMEM_LIMIT
        ),
        name="layer",
    )(*[pltpu.with_memory_space_constraint(v, pltpu.HBM) for v in (acts, gate, up, down, shrink, expand, row_adapter, page_table.reshape(1, -1))])


def solution(mesh):
    return jax.shard_map(
        on_device,
        mesh=mesh,
        in_specs=(
            P(None, None, "tp"),
            P("tp", "pool"),
            P("tp", "pool"),
            P("pool", "tp"),
            P("pool", None, "tp"),
            P("pool", "tp", None),
            P(),
            P(),
        ),
        out_specs=P(None, None, "tp"),
        check_vma=False,
    )
```

```python
import functools

import jax
import jax.numpy as jnp
from jax import lax
from jax.experimental import pallas as pl
from jax.experimental.pallas import tpu as pltpu
from jax.sharding import PartitionSpec as P

MESH = pl.DeviceIdType.MESH
F32 = jnp.float32
BF16 = jnp.bfloat16
adapter_scale = 2.0

NY, NZ, NX = 8, 8, 4
NPOOL = NZ * NX
FIRST, LAST = 6, 26
VMEM_LIMIT = 24 * 2**20


def mod(a, n):
    return lax.rem(a + n, n)


def remote(src, dst, ssem, rsem, device):
    return pltpu.make_async_remote_copy(
        src_ref=src, dst_ref=dst, send_sem=ssem, recv_sem=rsem, device_id=device, device_id_type=MESH
    )


def kernel(
    acts, gate, up, down, shrink, expand, row_ids, pages_at, out, rowad, ptab,
    aloc, apar, gown, gpar, uown, upar, dbuf, sbuf, ebuf, esel, epar, e8, blocks, wide,
    lroth, lrpar, lrs, lrr, lr8, lrx, lrz, gacc, uacc, gpart, upart, act,
    m4, m2, f3, f1, hid, xs, xr, zs, zr, zg, obuf,
    lsem, psend, precv, esend, erecv, lsend, lrecv, lxs, lxr, lzs, lzr, rsend, rrecv,
    hsend, hrecv, xsend, xrecv, zsend, zrecv, fsend, frecv, osend, orecv,
):
    rows = apar.shape[0]
    hidden = gown.shape[1]
    pages = expand.shape[0]
    piece = rows // NY
    part_rows = piece // 2
    half_rows = part_rows // 2
    p = lax.axis_index("pool")
    t = lax.axis_index("tp")
    c = lax.rem(t, 2)
    o = 1 - c
    y = t // 2
    z = p // NX
    x = lax.rem(p, NX)
    partner = (p, 2 * y + o)
    pending = []

    def go(src, dst, ssem, rsem, device):
        cp = remote(src, dst, ssem, rsem, device)
        cp.start()
        pending.append(cp)

    def come(src, dst, ssem, rsem):
        remote(src, dst, ssem, rsem, partner).wait_recv()

    def at_y(n):
        return (p, 2 * mod(y + n + NY, NY) + c)

    def at_z(n):
        return (mod(z + n, NZ) * NX + x, t)

    def at_x(n):
        return (z * NX + mod(x + n, NX), t)

    bar = pltpu.get_barrier_semaphore()

    def greet(n, carry):
        pl.semaphore_signal(bar, inc=1, device_id=(mod(p + n, NPOOL), t), device_id_type=MESH)
        return carry

    lax.fori_loop(1, NPOOL, greet, 0)
    for n in (4, 3, 5, 2, 6, 1, 7):
        pl.semaphore_signal(bar, inc=1, device_id=at_y(n), device_id_type=MESH)
    for n in range(1, NX):
        pl.semaphore_signal(
            bar, inc=1, device_id=(z * NX + mod(x + n, NX), 2 * y + o), device_id_type=MESH
        )
    pl.semaphore_signal(bar, inc=1, device_id=partner, device_id_type=MESH)

    loads = [
        pltpu.make_async_copy(shrink, sbuf, lsem.at[0]),
        pltpu.make_async_copy(acts, aloc, lsem.at[1]),
        pltpu.make_async_copy(expand, ebuf, lsem.at[2]),
        pltpu.make_async_copy(gate, gown, lsem.at[3]),
        pltpu.make_async_copy(up, uown, lsem.at[4]),
        pltpu.make_async_copy(down, dbuf.at[c], lsem.at[5]),
    ]
    small = [
        pltpu.make_async_copy(row_ids, rowad, lsem.at[6]),
        pltpu.make_async_copy(pages_at, ptab, lsem.at[7]),
    ]
    for cp in small:
        cp.start()
    for cp in loads:
        cp.start()

    for cp in small:
        cp.wait()
    table = jnp.broadcast_to(ptab[...].astype(F32).astype(BF16), (8, ptab.shape[1]))
    base = (p * pages).astype(F32)
    rel = []
    for m in range(2):
        ids = jnp.broadcast_to(rowad[m : m + 1, :], (ptab.shape[1], rows))
        hot = (lax.broadcasted_iota(jnp.int32, ids.shape, 0) == ids).astype(F32).astype(BF16)
        rel.append(jnp.dot(table, hot, preferred_element_type=F32) - base)
    rel_mine = jnp.where(c == 0, rel[0], rel[1])
    rel_other = jnp.where(c == 0, rel[1], rel[0])

    def used(r, j):
        return jnp.max(jnp.where(r == float(j), 1.0, 0.0), axis=1, keepdims=True)

    use_mine = [used(rel_mine, j) for j in range(pages)]
    use_other = [used(rel_other, j) for j in range(pages)]
    row_mask = (rel_mine[0:1, :] > -0.5) & (rel_mine[0:1, :] < pages - 0.5)

    loads[0].wait()
    loads[1].wait()

    def low_part(use, a):
        factor = jnp.zeros(sbuf.shape[1:], F32)
        for j in range(pages):
            factor = factor + sbuf[j].astype(F32) * use[j][0:1]
        return lax.dot_general(
            factor.astype(BF16), a, (((1,), (1,)), ((), ())), preferred_element_type=F32
        )

    low = low_part(use_mine, aloc[c])
    lroth[...] = low_part(use_other, aloc[o])

    loads[2].wait()
    chunk = 2048

    def pick(i, carry):
        cols = pl.ds(pl.multiple_of(i * chunk, chunk), chunk)
        mine = jnp.zeros((ebuf.shape[1], chunk), F32)
        other = jnp.zeros((ebuf.shape[1], chunk), F32)
        for j in range(pages):
            page = ebuf[j, :, cols].astype(F32)
            mine = mine + page * use_mine[j][:4]
            other = other + page * use_other[j][:4]
        esel[0, :, cols] = mine.astype(BF16)
        esel[1, :, cols] = other.astype(BF16)
        return carry

    lax.fori_loop(0, ebuf.shape[2] // chunk, pick, 0)

    for cp in loads[3:]:
        cp.wait()
    gacc[...] = jnp.dot(aloc[c], gown[...], preferred_element_type=F32)
    uacc[...] = jnp.dot(aloc[c], uown[...], preferred_element_type=F32)
    pl.semaphore_wait(bar, 1 + (NY - 1) + (NPOOL - 1) + (NX - 1))

    ex = [
        remote(lroth, lrpar, psend.at[0], precv.at[0], partner),
        remote(esel.at[1], epar, psend.at[1], precv.at[1], partner),
        remote(aloc.at[o], apar, psend.at[2], precv.at[2], partner),
        remote(gown, gpar, psend.at[3], precv.at[3], partner),
        remote(uown, upar, psend.at[4], precv.at[4], partner),
        remote(dbuf.at[c], dbuf.at[c], psend.at[5], precv.at[5], partner),
    ]
    for cp in ex:
        cp.start()

    ex[0].wait_recv()
    low = jnp.where(row_mask, low + lrpar[...], 0.0)
    for k in range(NY):
        lrs[k] = low[8 * k : 8 * k + 8, :]
    for n in (4, 3, 5, 2, 6, 1, 7):
        go(lrs.at[mod(y + n, NY)], lrr.at[n], lsend.at[n], lrecv.at[n], at_y(n))

    ex[1].wait_recv()

    def join(i, carry):
        cols = pl.ds(pl.multiple_of(i * chunk, chunk), chunk)
        a = esel[0, :, cols].astype(F32)
        b = epar[:, cols].astype(F32)
        e8[:, cols] = jnp.concatenate(
            [jnp.where(c == 0, a, b), jnp.where(c == 0, b, a)], axis=0
        ).astype(BF16)
        return carry

    lax.fori_loop(0, ebuf.shape[2] // chunk, join, 0)

    def block_to(n):
        q = mod(p + n, NPOOL)
        return remote(
            e8.at[:, pl.ds(pl.multiple_of(q * hidden, 128), hidden)],
            blocks.at[p],
            esend.at[n],
            erecv.at[p],
            (q, t),
        )

    def send_block(n, carry):
        block_to(n).start()
        return carry

    lax.fori_loop(FIRST, LAST, send_block, 0)
    blocks[p] = e8[:, pl.ds(pl.multiple_of(p * hidden, 128), hidden)]

    def own_rows(dest, first, count):
        return pl.ds(pl.multiple_of(dest * piece + first, 8), count)

    def spans(s, h):
        near = h * part_rows + s * half_rows
        far = h * part_rows + (1 - s) * half_rows
        return near, far

    def sum_first(q, part, h):
        for s in range(2):
            d = 1 - 2 * s
            near, far = spans(s, h)
            go(
                part.at[mod(y + 4, NY), near : near + half_rows],
                m4.at[q, s, h],
                rsend.at[q, 0, s, h],
                rrecv.at[q, 0, s, h],
                at_y(d),
            )
            go(
                part.at[mod(y + 2 * d + NY, NY), h * part_rows : (h + 1) * part_rows],
                m2.at[q, s, h],
                rsend.at[q, 1, s, h],
                rrecv.at[q, 1, s, h],
                at_y(d),
            )

    def sum_direct(q, part, h):
        for s in range(2):
            d = 1 - 2 * s
            near, far = spans(s, h)
            go(
                part.at[mod(y + 3 * d + NY, NY), far : far + half_rows],
                f3.at[q, s, far : far + half_rows],
                rsend.at[q, 2, s, h],
                rrecv.at[q, 2, s, h],
                at_y(3 * d),
            )

    def sum_second(q, part, acc, h):
        for s in range(2):
            d = 1 - 2 * s
            near, far = spans(s, h)
            dest = mod(y + 3 * d + NY, NY)
            come(m4.at[q, s, h], m4.at[q, s, h], rsend.at[q, 0, s, h], rrecv.at[q, 0, s, h])
            part[dest, near : near + half_rows, :] = (
                acc[own_rows(dest, near, half_rows), :] + m4[q, s, h].astype(F32)
            ).astype(BF16)
            go(
                part.at[dest, near : near + half_rows],
                f3.at[q, s, near : near + half_rows],
                rsend.at[q, 3, s, h],
                rrecv.at[q, 3, s, h],
                at_y(3 * d),
            )
        for s in range(2):
            d = 1 - 2 * s
            dest = mod(y + d + NY, NY)
            come(m2.at[q, s, h], m2.at[q, s, h], rsend.at[q, 1, s, h], rrecv.at[q, 1, s, h])
            part[dest, h * part_rows : (h + 1) * part_rows, :] = (
                acc[own_rows(dest, h * part_rows, part_rows), :] + m2[q, s, h].astype(F32)
            ).astype(BF16)
            go(
                part.at[dest, h * part_rows : (h + 1) * part_rows],
                f1.at[q, s, h],
                rsend.at[q, 4, s, h],
                rrecv.at[q, 4, s, h],
                at_y(d),
            )

    def sum_last(q, acc, h):
        total = acc[own_rows(y, h * part_rows, part_rows), :]
        span = slice(h * part_rows, (h + 1) * part_rows)
        for s in range(2):
            near, far = spans(s, h)
            a = f3.at[q, s, far : far + half_rows]
            b = f3.at[q, s, near : near + half_rows]
            come(a, a, rsend.at[q, 2, s, h], rrecv.at[q, 2, s, h])
            come(b, b, rsend.at[q, 3, s, h], rrecv.at[q, 3, s, h])
            come(f1.at[q, s, h], f1.at[q, s, h], rsend.at[q, 4, s, h], rrecv.at[q, 4, s, h])
            total = total + f3[q, s, span, :].astype(F32) + f1[q, s, h].astype(F32)
        return total

    ex[2].wait_recv()
    ex[3].wait_recv()
    gacc[...] += jnp.dot(apar[...], gpar[...], preferred_element_type=F32)
    gpart[...] = gacc[...].astype(BF16).reshape(gpart.shape)
    for h in range(2):
        sum_first(0, gpart, h)
    for h in range(2):
        sum_direct(0, gpart, h)

    total = lrs[y]
    for n in range(1, NY):
        come(lrs.at[0], lrr.at[n], lsend.at[n], lrecv.at[n])
        total = total + lrr[n]
    lr8[0] = total.astype(BF16)
    for k in (2, 1, 3):
        go(lr8.at[0], lrx.at[k], lxs.at[k], lxr.at[k], at_x(k))

    for h in range(2):
        sum_second(0, gpart, gacc, h)

    total = lr8[0].astype(F32)
    for k in range(1, NX):
        come(lr8.at[0], lrx.at[k], lxs.at[k], lxr.at[k])
        total = total + lrx[k].astype(F32)
    lr8[1] = total.astype(BF16)
    for k in (4, 3, 5, 2, 6, 1, 7):
        go(lr8.at[1], lrz.at[k], lzs.at[k], lzr.at[k], at_z(k))
    lax.fori_loop(1, FIRST, send_block, 0)
    lax.fori_loop(LAST, NPOOL, send_block, 0)

    ex[4].wait_recv()
    uacc[...] += jnp.dot(apar[...], upar[...], preferred_element_type=F32)

    total = lr8[1].astype(F32)
    for k in range(1, NZ):
        come(lr8.at[1], lrz.at[k], lzs.at[k], lzr.at[k])
        total = total + lrz[k].astype(F32)
    page = rel_mine + base
    for q in range(NPOOL):
        owned = (page > q * pages - 0.5) & (page < (q + 1) * pages - 0.5)
        wide[q] = jnp.where(owned, total, 0.0).astype(BF16)

    for h in range(2):
        g = sum_last(0, gacc, h)
        act[h * part_rows : (h + 1) * part_rows, :] = g / (1.0 + jnp.exp(-g))

    def arrived(n, carry):
        q = mod(p + n, NPOOL)
        remote(e8.at[:, pl.ds(0, hidden)], blocks.at[q], esend.at[n], erecv.at[q], (q, t)).wait_recv()
        return carry

    lax.fori_loop(1, NPOOL, arrived, 0)
    wide_all = wide[...].reshape(NPOOL * 8, rows)
    block_all = blocks[...].reshape(NPOOL * 8, hidden)
    uacc[...] += adapter_scale * lax.dot_general(
        wide_all, block_all, (((0,), (0,)), ((), ())), preferred_element_type=F32
    )
    upart[...] = uacc[...].astype(BF16).reshape(upart.shape)
    for h in range(2):
        sum_first(1, upart, h)
    for h in range(2):
        sum_direct(1, upart, h)
    for h in range(2):
        sum_second(1, upart, uacc, h)

    def share_first(h):
        span = slice(h * part_rows, (h + 1) * part_rows)
        hid[0, span, :] = (act[span, :] * sum_last(1, uacc, h)).astype(BF16)
        for s in range(2):
            d = 1 - 2 * s
            one, three = (1, 3) if s == 0 else (7, 5)
            go(
                hid.at[0, span], hid.at[one, span],
                hsend.at[0, s, h], hrecv.at[0, s, h], at_y(d),
            )
            go(
                hid.at[0, span], hid.at[three, span],
                hsend.at[1, s, h], hrecv.at[1, s, h], at_y(3 * d),
            )

    def share_near(h):
        span = slice(h * part_rows, (h + 1) * part_rows)
        for s in range(2):
            d = 1 - 2 * s
            one, two = (1, 2) if s == 0 else (7, 6)
            come(hid.at[one, span], hid.at[one, span], hsend.at[0, s, h], hrecv.at[0, s, h])
            go(
                hid.at[one, span], hid.at[two, span],
                hsend.at[2, s, h], hrecv.at[2, s, h], at_y(d),
            )

    def share_far(h):
        span = slice(h * part_rows, (h + 1) * part_rows)
        for s in range(2):
            d = 1 - 2 * s
            three = 3 if s == 0 else 5
            near, far = spans(s, h)
            come(hid.at[three, span], hid.at[three, span], hsend.at[1, s, h], hrecv.at[1, s, h])
            go(
                hid.at[three, near : near + half_rows], hid.at[4, near : near + half_rows],
                hsend.at[3, s, h], hrecv.at[3, s, h], at_y(d),
            )

    def shared(n):
        for h in range(2):
            span = slice(h * part_rows, (h + 1) * part_rows)
            if n in (2, 6):
                s = 0 if n == 2 else 1
                come(hid.at[n, span], hid.at[n, span], hsend.at[2, s, h], hrecv.at[2, s, h])
            if n == 4:
                for s in range(2):
                    near, far = spans(s, h)
                    v = hid.at[4, near : near + half_rows]
                    come(v, v, hsend.at[3, s, h], hrecv.at[3, s, h])

    for h in range(2):
        share_first(h)

    ex[5].wait_recv()
    cols = xs.shape[3]

    def down_piece(n):
        shared(n)
        for half in range(2):
            part = jnp.dot(hid[n], dbuf[half], preferred_element_type=F32).astype(BF16)
            xs[n, 2 * half] = part[:, :cols]
            xs[n, 2 * half + 1] = part[:, cols:]
        for k in (2, 1, 3):
            go(xs.at[n, mod(x + k, NX)], xr.at[n, k], xsend.at[n, k], xrecv.at[n, k], at_x(k))

    def x_done(n):
        total = xs[n, x].astype(F32)
        for k in (1, 2, 3):
            come(xs.at[n, 0], xr.at[n, k], xsend.at[n, k], xrecv.at[n, k])
            total = total + xr[n, k].astype(F32)
        zs[n] = total.astype(BF16)
        owner = mod(y - n + NY, NY)

        @pl.when(owner == z)
        def _():
            zr[z] = zs[n]

        @pl.when(owner != z)
        def _():
            remote(zs.at[n], zr.at[z], zsend.at[n], zrecv.at[z], (owner * NX + x, t)).start()

    down_piece(0)
    for h in range(2):
        share_near(h)
    order = (0, 1, 7, 3, 5, 2, 6, 4)
    for i, n in enumerate(order):
        if n > 0:
            down_piece(n)
        if n == 7:
            for h in range(2):
                share_far(h)
        if i >= 7:
            x_done(order[i - 7])
    for n in order[-7:]:
        x_done(n)

    total = zr[z].astype(F32)
    for k in range(1, NZ):
        q = mod(z + k, NZ)
        come(zs.at[0], zr.at[q], zsend.at[0], zrecv.at[q])
        total = total + zr[q].astype(F32)

    def block_rows(k):
        return pl.ds(pl.multiple_of(mod(z - k + NZ, NZ) * piece, piece), piece)

    here = block_rows(0)
    zg[here, :] = total.astype(BF16)
    for k in (4, 3, 5, 2, 6, 1, 7):
        go(zg.at[here], zg.at[here], fsend.at[k], frecv.at[k], at_z(k))

    side = x // 2
    odd = lax.rem(x, 2)
    place = pl.ds(pl.multiple_of(odd * cols, cols), cols)
    for k in (0, 1, 7, 2, 6, 3, 5, 4):
        there = block_rows(k)
        if k > 0:
            come(zg.at[here], zg.at[there], fsend.at[k], frecv.at[k])
        slot = mod(z - k + NZ, NZ)
        for n in (2, 1, 3):
            go(
                zg.at[there],
                obuf.at[c, there, place],
                osend.at[k, n],
                orecv.at[odd, c, slot],
                (z * NX + mod(x + n, NX), 2 * y + side),
            )

        @pl.when(side != c)
        def _():
            remote(
                zg.at[there], obuf.at[c, there, place], osend.at[k, 0], orecv.at[odd, c, slot], partner
            ).start()

        @pl.when(side == c)
        def _():
            obuf[c, there, place] = zg[there, :]

    for a in range(2):
        for m in range(2):

            @pl.when(jnp.logical_or(2 * c + a != x, m != c))
            def _():
                for k in range(NZ):
                    v = obuf.at[m, k * piece : (k + 1) * piece, a * cols : (a + 1) * cols]
                    come(v, v, osend.at[0, 0], orecv.at[a, m, k])

    final = pltpu.make_async_copy(obuf, out, lsem.at[8])
    final.start()

    for cp in ex + pending:
        cp.wait_send()

    def left(n, carry):
        block_to(n).wait_send()
        return carry

    lax.fori_loop(1, NPOOL, left, 0)
    for n in range(NY):

        @pl.when(mod(y - n + NY, NY) != z)
        def _():
            remote(zs.at[n], zr.at[0], zsend.at[n], zrecv.at[0], at_z(1)).wait_send()

    @pl.when(side != c)
    def _():
        for k in range(NZ):
            remote(
                zg.at[here], obuf.at[c, here, place], osend.at[k, 0], orecv.at[0, 0, 0], partner
            ).wait_send()

    final.wait()


def on_device(acts, gate, up, down, shrink, expand, row_adapter, page_table):
    batches, rows, width = acts.shape
    hidden = gate.shape[1]
    out_width = down.shape[1]
    pages, rank, _ = shrink.shape
    rank_local, ff = expand.shape[1:]
    piece = rows // NY
    cols = 2 * out_width // NX
    anyspec = pl.BlockSpec(memory_space=pl.ANY)
    dma = pltpu.SemaphoreType.DMA
    ranks = 2 * rank_local
    scratch = [
        pltpu.VMEM(row_adapter.shape, jnp.int32),
        pltpu.VMEM((1, page_table.shape[0]), jnp.int32),
        pltpu.VMEM((2, rows, width), BF16),
        pltpu.VMEM((rows, width), BF16),
        pltpu.VMEM((width, hidden), BF16),
        pltpu.VMEM((width, hidden), BF16),
        pltpu.VMEM((width, hidden), BF16),
        pltpu.VMEM((width, hidden), BF16),
        pltpu.VMEM((2, hidden, out_width), BF16),
        pltpu.VMEM((pages, rank, width), BF16),
        pltpu.VMEM((pages, rank_local, ff), BF16),
        pltpu.VMEM((2, rank_local, ff), BF16),
        pltpu.VMEM((rank_local, ff), BF16),
        pltpu.VMEM((ranks, ff), BF16),
        pltpu.VMEM((NPOOL, ranks, hidden), BF16),
        pltpu.VMEM((NPOOL, ranks, rows), BF16),
        pltpu.VMEM((rank, rows), F32),
        pltpu.VMEM((rank, rows), F32),
        pltpu.VMEM((NY, ranks, rows), F32),
        pltpu.VMEM((NY, ranks, rows), F32),
        pltpu.VMEM((2, ranks, rows), BF16),
        pltpu.VMEM((NX, ranks, rows), BF16),
        pltpu.VMEM((NZ, ranks, rows), BF16),
        pltpu.VMEM((rows, hidden), F32),
        pltpu.VMEM((rows, hidden), F32),
        pltpu.VMEM((NY, piece, hidden), BF16),
        pltpu.VMEM((NY, piece, hidden), BF16),
        pltpu.VMEM((piece, hidden), F32),
        pltpu.VMEM((2, 2, 2, piece // 4, hidden), BF16),
        pltpu.VMEM((2, 2, 2, piece // 2, hidden), BF16),
        pltpu.VMEM((2, 2, piece, hidden), BF16),
        pltpu.VMEM((2, 2, 2, piece // 2, hidden), BF16),
        pltpu.VMEM((NY, piece, hidden), BF16),
        pltpu.VMEM((NY, NX, piece, cols), BF16),
        pltpu.VMEM((NY, NX, piece, cols), BF16),
        pltpu.VMEM((NY, piece, cols), BF16),
        pltpu.VMEM((NZ, piece, cols), BF16),
        pltpu.VMEM((rows, cols), BF16),
        pltpu.VMEM((batches, rows, out_width), BF16),
        dma((9,)),
        dma((6,)), dma((6,)),
        dma((NPOOL,)), dma((NPOOL,)),
        dma((NY,)), dma((NY,)),
        dma((NX,)), dma((NX,)),
        dma((NZ,)), dma((NZ,)),
        dma((2, 5, 2, 2)), dma((2, 5, 2, 2)),
        dma((4, 2, 2)), dma((4, 2, 2)),
        dma((NY, NX)), dma((NY, NX)),
        dma((NY,)), dma((NZ,)),
        dma((NZ,)), dma((NZ,)),
        dma((NZ, NX)), dma((2, 2, NZ)),
    ]
    return pl.pallas_call(
        kernel,
        out_shape=jax.ShapeDtypeStruct((batches, rows, out_width), BF16),
        in_specs=[anyspec] * 8,
        out_specs=anyspec,
        scratch_shapes=scratch,
        compiler_params=pltpu.CompilerParams(
            collective_id=0, has_side_effects=True, vmem_limit_bytes=VMEM_LIMIT
        ),
        name="layer",
    )(*[pltpu.with_memory_space_constraint(v, pltpu.HBM) for v in (acts, gate, up, down, shrink, expand, row_adapter, page_table.reshape(1, -1))])


def solution(mesh):
    return jax.shard_map(
        on_device,
        mesh=mesh,
        in_specs=(
            P(None, None, "tp"),
            P("tp", "pool"),
            P("tp", "pool"),
            P("pool", "tp"),
            P("pool", None, "tp"),
            P("pool", "tp", None),
            P(),
            P(),
        ),
        out_specs=P(None, None, "tp"),
        check_vma=False,
    )
```

```python
import functools

import jax
import jax.numpy as jnp
from jax import lax
from jax.experimental import pallas as pl
from jax.experimental.pallas import tpu as pltpu
from jax.sharding import PartitionSpec as P

MESH = pl.DeviceIdType.MESH
F32 = jnp.float32
BF16 = jnp.bfloat16
adapter_scale = 2.0

NY, NZ, NX = 8, 8, 4
NPOOL = NZ * NX
FIRST, LAST = 6, 26
VMEM_LIMIT = 24 * 2**20


def mod(a, n):
    return lax.rem(a + n, n)


def remote(src, dst, ssem, rsem, device):
    return pltpu.make_async_remote_copy(
        src_ref=src, dst_ref=dst, send_sem=ssem, recv_sem=rsem, device_id=device, device_id_type=MESH
    )


def kernel(
    acts, gate, up, down, shrink, expand, row_ids, pages_at, out, rowad, ptab,
    aloc, apar, gown, gpar, uown, upar, dbuf, sbuf, ebuf, esel, epar, e8, blocks, wide,
    lroth, lrpar, lrs, lrr, lr8, lrx, lrz, gacc, uacc, gpart, upart, act,
    m4, m2, f3, f1, hid, xs, xr, zs, zr, zg, obuf,
    lsem, psend, precv, esend, erecv, lsend, lrecv, lxs, lxr, lzs, lzr, rsend, rrecv,
    hsend, hrecv, xsend, xrecv, zsend, zrecv, fsend, frecv, osend, orecv,
):
    rows = apar.shape[0]
    hidden = gown.shape[1]
    pages = expand.shape[0]
    piece = rows // NY
    part_rows = piece // 2
    half_rows = part_rows // 2
    p = lax.axis_index("pool")
    t = lax.axis_index("tp")
    c = lax.rem(t, 2)
    o = 1 - c
    y = t // 2
    z = p // NX
    x = lax.rem(p, NX)
    partner = (p, 2 * y + o)
    pending = []

    def go(src, dst, ssem, rsem, device):
        cp = remote(src, dst, ssem, rsem, device)
        cp.start()
        pending.append(cp)

    def come(src, dst, ssem, rsem):
        remote(src, dst, ssem, rsem, partner).wait_recv()

    def at_y(n):
        return (p, 2 * mod(y + n + NY, NY) + c)

    def at_z(n):
        return (mod(z + n, NZ) * NX + x, t)

    def at_x(n):
        return (z * NX + mod(x + n, NX), t)

    bar = pltpu.get_barrier_semaphore()

    def greet(n, carry):
        pl.semaphore_signal(bar, inc=1, device_id=(mod(p + n, NPOOL), t), device_id_type=MESH)
        return carry

    lax.fori_loop(1, NPOOL, greet, 0)
    for n in (4, 3, 5, 2, 6, 1, 7):
        pl.semaphore_signal(bar, inc=1, device_id=at_y(n), device_id_type=MESH)
    for n in range(1, NX):
        pl.semaphore_signal(
            bar, inc=1, device_id=(z * NX + mod(x + n, NX), 2 * y + o), device_id_type=MESH
        )
    pl.semaphore_signal(bar, inc=1, device_id=partner, device_id_type=MESH)

    loads = [
        pltpu.make_async_copy(shrink, sbuf, lsem.at[0]),
        pltpu.make_async_copy(acts, aloc, lsem.at[1]),
        pltpu.make_async_copy(expand, ebuf, lsem.at[2]),
        pltpu.make_async_copy(gate, gown, lsem.at[3]),
        pltpu.make_async_copy(up, uown, lsem.at[4]),
        pltpu.make_async_copy(down, dbuf.at[c], lsem.at[5]),
    ]
    small = [
        pltpu.make_async_copy(row_ids, rowad, lsem.at[6]),
        pltpu.make_async_copy(pages_at, ptab, lsem.at[7]),
    ]
    for cp in small:
        cp.start()
    for cp in loads:
        cp.start()

    for cp in small:
        cp.wait()
    table = jnp.broadcast_to(ptab[...].astype(F32).astype(BF16), (8, ptab.shape[1]))
    base = (p * pages).astype(F32)
    rel = []
    for m in range(2):
        ids = jnp.broadcast_to(rowad[m : m + 1, :], (ptab.shape[1], rows))
        hot = (lax.broadcasted_iota(jnp.int32, ids.shape, 0) == ids).astype(F32).astype(BF16)
        rel.append(jnp.dot(table, hot, preferred_element_type=F32) - base)
    rel_mine = jnp.where(c == 0, rel[0], rel[1])
    rel_other = jnp.where(c == 0, rel[1], rel[0])

    def used(r, j):
        return jnp.max(jnp.where(r == float(j), 1.0, 0.0), axis=1, keepdims=True)

    use_mine = [used(rel_mine, j) for j in range(pages)]
    use_other = [used(rel_other, j) for j in range(pages)]
    row_mask = (rel_mine[0:1, :] > -0.5) & (rel_mine[0:1, :] < pages - 0.5)

    loads[0].wait()
    loads[1].wait()

    def low_part(use, a):
        factor = jnp.zeros(sbuf.shape[1:], F32)
        for j in range(pages):
            factor = factor + sbuf[j].astype(F32) * use[j][0:1]
        return lax.dot_general(
            factor.astype(BF16), a, (((1,), (1,)), ((), ())), preferred_element_type=F32
        )

    low = low_part(use_mine, aloc[c])
    lroth[...] = low_part(use_other, aloc[o])

    loads[2].wait()
    chunk = 2048

    def pick(i, carry):
        cols = pl.ds(pl.multiple_of(i * chunk, chunk), chunk)
        mine = jnp.zeros((ebuf.shape[1], chunk), F32)
        other = jnp.zeros((ebuf.shape[1], chunk), F32)
        for j in range(pages):
            page = ebuf[j, :, cols].astype(F32)
            mine = mine + page * use_mine[j][:4]
            other = other + page * use_other[j][:4]
        esel[0, :, cols] = mine.astype(BF16)
        esel[1, :, cols] = other.astype(BF16)
        return carry

    lax.fori_loop(0, ebuf.shape[2] // chunk, pick, 0)

    for cp in loads[3:]:
        cp.wait()
    gacc[...] = jnp.dot(aloc[c], gown[...], preferred_element_type=F32)
    uacc[...] = jnp.dot(aloc[c], uown[...], preferred_element_type=F32)
    pl.semaphore_wait(bar, 1 + (NY - 1) + (NPOOL - 1) + (NX - 1))

    ex = [
        remote(lroth, lrpar, psend.at[0], precv.at[0], partner),
        remote(esel.at[1], epar, psend.at[1], precv.at[1], partner),
        remote(aloc.at[o], apar, psend.at[2], precv.at[2], partner),
        remote(gown, gpar, psend.at[3], precv.at[3], partner),
        remote(uown, upar, psend.at[4], precv.at[4], partner),
        remote(dbuf.at[c], dbuf.at[c], psend.at[5], precv.at[5], partner),
    ]
    for cp in ex:
        cp.start()

    ex[0].wait_recv()
    low = jnp.where(row_mask, low + lrpar[...], 0.0)
    for k in range(NY):
        lrs[k] = low[8 * k : 8 * k + 8, :]
    for n in (4, 3, 5, 2, 6, 1, 7):
        go(lrs.at[mod(y + n, NY)], lrr.at[n], lsend.at[n], lrecv.at[n], at_y(n))

    ex[1].wait_recv()

    def join(i, carry):
        cols = pl.ds(pl.multiple_of(i * chunk, chunk), chunk)
        a = esel[0, :, cols].astype(F32)
        b = epar[:, cols].astype(F32)
        e8[:, cols] = jnp.concatenate(
            [jnp.where(c == 0, a, b), jnp.where(c == 0, b, a)], axis=0
        ).astype(BF16)
        return carry

    lax.fori_loop(0, ebuf.shape[2] // chunk, join, 0)

    def block_to(n):
        q = mod(p + n, NPOOL)
        return remote(
            e8.at[:, pl.ds(pl.multiple_of(q * hidden, 128), hidden)],
            blocks.at[p],
            esend.at[n],
            erecv.at[p],
            (q, t),
        )

    def send_block(n, carry):
        block_to(n).start()
        return carry

    lax.fori_loop(FIRST, LAST, send_block, 0)
    blocks[p] = e8[:, pl.ds(pl.multiple_of(p * hidden, 128), hidden)]

    def own_rows(dest, first, count):
        return pl.ds(pl.multiple_of(dest * piece + first, 8), count)

    def spans(s, h):
        near = h * part_rows + s * half_rows
        far = h * part_rows + (1 - s) * half_rows
        return near, far

    def sum_first(q, part, h):
        for s in range(2):
            d = 1 - 2 * s
            near, far = spans(s, h)
            go(
                part.at[mod(y + 4, NY), near : near + half_rows],
                m4.at[q, s, h],
                rsend.at[q, 0, s, h],
                rrecv.at[q, 0, s, h],
                at_y(d),
            )
            go(
                part.at[mod(y + 2 * d + NY, NY), h * part_rows : (h + 1) * part_rows],
                m2.at[q, s, h],
                rsend.at[q, 1, s, h],
                rrecv.at[q, 1, s, h],
                at_y(d),
            )

    def sum_direct(q, part, h):
        for s in range(2):
            d = 1 - 2 * s
            near, far = spans(s, h)
            go(
                part.at[mod(y + 3 * d + NY, NY), far : far + half_rows],
                f3.at[q, s, far : far + half_rows],
                rsend.at[q, 2, s, h],
                rrecv.at[q, 2, s, h],
                at_y(3 * d),
            )

    def sum_second(q, part, acc, h):
        for s in range(2):
            d = 1 - 2 * s
            near, far = spans(s, h)
            dest = mod(y + 3 * d + NY, NY)
            come(m4.at[q, s, h], m4.at[q, s, h], rsend.at[q, 0, s, h], rrecv.at[q, 0, s, h])
            part[dest, near : near + half_rows, :] = (
                acc[own_rows(dest, near, half_rows), :] + m4[q, s, h].astype(F32)
            ).astype(BF16)
            go(
                part.at[dest, near : near + half_rows],
                f3.at[q, s, near : near + half_rows],
                rsend.at[q, 3, s, h],
                rrecv.at[q, 3, s, h],
                at_y(3 * d),
            )
        for s in range(2):
            d = 1 - 2 * s
            dest = mod(y + d + NY, NY)
            come(m2.at[q, s, h], m2.at[q, s, h], rsend.at[q, 1, s, h], rrecv.at[q, 1, s, h])
            part[dest, h * part_rows : (h + 1) * part_rows, :] = (
                acc[own_rows(dest, h * part_rows, part_rows), :] + m2[q, s, h].astype(F32)
            ).astype(BF16)
            go(
                part.at[dest, h * part_rows : (h + 1) * part_rows],
                f1.at[q, s, h],
                rsend.at[q, 4, s, h],
                rrecv.at[q, 4, s, h],
                at_y(d),
            )

    def sum_last(q, acc, h):
        total = acc[own_rows(y, h * part_rows, part_rows), :]
        span = slice(h * part_rows, (h + 1) * part_rows)
        for s in range(2):
            near, far = spans(s, h)
            a = f3.at[q, s, far : far + half_rows]
            b = f3.at[q, s, near : near + half_rows]
            come(a, a, rsend.at[q, 2, s, h], rrecv.at[q, 2, s, h])
            come(b, b, rsend.at[q, 3, s, h], rrecv.at[q, 3, s, h])
            come(f1.at[q, s, h], f1.at[q, s, h], rsend.at[q, 4, s, h], rrecv.at[q, 4, s, h])
            total = total + f3[q, s, span, :].astype(F32) + f1[q, s, h].astype(F32)
        return total

    ex[2].wait_recv()
    ex[3].wait_recv()
    gacc[...] += jnp.dot(apar[...], gpar[...], preferred_element_type=F32)
    gpart[...] = gacc[...].astype(BF16).reshape(gpart.shape)
    for h in range(2):
        sum_first(0, gpart, h)
    for h in range(2):
        sum_direct(0, gpart, h)

    total = lrs[y]
    for n in range(1, NY):
        come(lrs.at[0], lrr.at[n], lsend.at[n], lrecv.at[n])
        total = total + lrr[n]
    lr8[0] = total.astype(BF16)
    for k in (2, 1, 3):
        go(lr8.at[0], lrx.at[k], lxs.at[k], lxr.at[k], at_x(k))

    total = lr8[0].astype(F32)
    for k in range(1, NX):
        come(lr8.at[0], lrx.at[k], lxs.at[k], lxr.at[k])
        total = total + lrx[k].astype(F32)
    lr8[1] = total.astype(BF16)
    for k in (4, 3, 5, 2, 6, 1, 7):
        go(lr8.at[1], lrz.at[k], lzs.at[k], lzr.at[k], at_z(k))
    lax.fori_loop(1, FIRST, send_block, 0)
    lax.fori_loop(LAST, NPOOL, send_block, 0)

    for h in range(2):
        sum_second(0, gpart, gacc, h)

    ex[4].wait_recv()
    uacc[...] += jnp.dot(apar[...], upar[...], preferred_element_type=F32)

    total = lr8[1].astype(F32)
    for k in range(1, NZ):
        come(lr8.at[1], lrz.at[k], lzs.at[k], lzr.at[k])
        total = total + lrz[k].astype(F32)
    page = rel_mine + base
    for q in range(NPOOL):
        owned = (page > q * pages - 0.5) & (page < (q + 1) * pages - 0.5)
        wide[q] = jnp.where(owned, total, 0.0).astype(BF16)

    for h in range(2):
        g = sum_last(0, gacc, h)
        act[h * part_rows : (h + 1) * part_rows, :] = g / (1.0 + jnp.exp(-g))

    def arrived(n, carry):
        q = mod(p + n, NPOOL)
        remote(e8.at[:, pl.ds(0, hidden)], blocks.at[q], esend.at[n], erecv.at[q], (q, t)).wait_recv()
        return carry

    lax.fori_loop(1, NPOOL, arrived, 0)
    wide_all = wide[...].reshape(NPOOL * 8, rows)
    block_all = blocks[...].reshape(NPOOL * 8, hidden)
    uacc[...] += adapter_scale * lax.dot_general(
        wide_all, block_all, (((0,), (0,)), ((), ())), preferred_element_type=F32
    )
    upart[...] = uacc[...].astype(BF16).reshape(upart.shape)
    for h in range(2):
        sum_first(1, upart, h)
    for h in range(2):
        sum_direct(1, upart, h)
    for h in range(2):
        sum_second(1, upart, uacc, h)

    def share_first(h):
        span = slice(h * part_rows, (h + 1) * part_rows)
        hid[0, span, :] = (act[span, :] * sum_last(1, uacc, h)).astype(BF16)
        for s in range(2):
            d = 1 - 2 * s
            one, three = (1, 3) if s == 0 else (7, 5)
            go(
                hid.at[0, span], hid.at[one, span],
                hsend.at[0, s, h], hrecv.at[0, s, h], at_y(d),
            )
            go(
                hid.at[0, span], hid.at[three, span],
                hsend.at[1, s, h], hrecv.at[1, s, h], at_y(3 * d),
            )

    def share_near(h):
        span = slice(h * part_rows, (h + 1) * part_rows)
        for s in range(2):
            d = 1 - 2 * s
            one, two = (1, 2) if s == 0 else (7, 6)
            come(hid.at[one, span], hid.at[one, span], hsend.at[0, s, h], hrecv.at[0, s, h])
            go(
                hid.at[one, span], hid.at[two, span],
                hsend.at[2, s, h], hrecv.at[2, s, h], at_y(d),
            )

    def share_far(h):
        span = slice(h * part_rows, (h + 1) * part_rows)
        for s in range(2):
            d = 1 - 2 * s
            three = 3 if s == 0 else 5
            near, far = spans(s, h)
            come(hid.at[three, span], hid.at[three, span], hsend.at[1, s, h], hrecv.at[1, s, h])
            go(
                hid.at[three, near : near + half_rows], hid.at[4, near : near + half_rows],
                hsend.at[3, s, h], hrecv.at[3, s, h], at_y(d),
            )

    def shared(n):
        for h in range(2):
            span = slice(h * part_rows, (h + 1) * part_rows)
            if n in (2, 6):
                s = 0 if n == 2 else 1
                come(hid.at[n, span], hid.at[n, span], hsend.at[2, s, h], hrecv.at[2, s, h])
            if n == 4:
                for s in range(2):
                    near, far = spans(s, h)
                    v = hid.at[4, near : near + half_rows]
                    come(v, v, hsend.at[3, s, h], hrecv.at[3, s, h])

    for h in range(2):
        share_first(h)

    ex[5].wait_recv()
    cols = xs.shape[3]

    def down_piece(n):
        shared(n)
        for half in range(2):
            part = jnp.dot(hid[n], dbuf[half], preferred_element_type=F32).astype(BF16)
            xs[n, 2 * half] = part[:, :cols]
            xs[n, 2 * half + 1] = part[:, cols:]
        for k in (2, 1, 3):
            go(xs.at[n, mod(x + k, NX)], xr.at[n, k], xsend.at[n, k], xrecv.at[n, k], at_x(k))

    def x_done(n):
        total = xs[n, x].astype(F32)
        for k in (1, 2, 3):
            come(xs.at[n, 0], xr.at[n, k], xsend.at[n, k], xrecv.at[n, k])
            total = total + xr[n, k].astype(F32)
        zs[n] = total.astype(BF16)
        owner = mod(y - n + NY, NY)

        @pl.when(owner == z)
        def _():
            zr[z] = zs[n]

        @pl.when(owner != z)
        def _():
            remote(zs.at[n], zr.at[z], zsend.at[n], zrecv.at[z], (owner * NX + x, t)).start()

    down_piece(0)
    for h in range(2):
        share_near(h)
    order = (0, 1, 7, 3, 5, 2, 6, 4)
    for i, n in enumerate(order):
        if n > 0:
            down_piece(n)
        if n == 7:
            for h in range(2):
                share_far(h)
        if i >= 7:
            x_done(order[i - 7])
    for n in order[-7:]:
        x_done(n)

    total = zr[z].astype(F32)
    for k in range(1, NZ):
        q = mod(z + k, NZ)
        come(zs.at[0], zr.at[q], zsend.at[0], zrecv.at[q])
        total = total + zr[q].astype(F32)

    def block_rows(k):
        return pl.ds(pl.multiple_of(mod(z - k + NZ, NZ) * piece, piece), piece)

    here = block_rows(0)
    zg[here, :] = total.astype(BF16)
    for k in (4, 3, 5, 2, 6, 1, 7):
        go(zg.at[here], zg.at[here], fsend.at[k], frecv.at[k], at_z(k))

    side = x // 2
    odd = lax.rem(x, 2)
    place = pl.ds(pl.multiple_of(odd * cols, cols), cols)
    for k in (0, 1, 7, 2, 6, 3, 5, 4):
        there = block_rows(k)
        if k > 0:
            come(zg.at[here], zg.at[there], fsend.at[k], frecv.at[k])
        slot = mod(z - k + NZ, NZ)
        for n in (2, 1, 3):
            go(
                zg.at[there],
                obuf.at[c, there, place],
                osend.at[k, n],
                orecv.at[odd, c, slot],
                (z * NX + mod(x + n, NX), 2 * y + side),
            )

        @pl.when(side != c)
        def _():
            remote(
                zg.at[there], obuf.at[c, there, place], osend.at[k, 0], orecv.at[odd, c, slot], partner
            ).start()

        @pl.when(side == c)
        def _():
            obuf[c, there, place] = zg[there, :]

    for a in range(2):
        for m in range(2):

            @pl.when(jnp.logical_or(2 * c + a != x, m != c))
            def _():
                for k in range(NZ):
                    v = obuf.at[m, k * piece : (k + 1) * piece, a * cols : (a + 1) * cols]
                    come(v, v, osend.at[0, 0], orecv.at[a, m, k])

    final = pltpu.make_async_copy(obuf, out, lsem.at[8])
    final.start()

    for cp in ex + pending:
        cp.wait_send()

    def left(n, carry):
        block_to(n).wait_send()
        return carry

    lax.fori_loop(1, NPOOL, left, 0)
    for n in range(NY):

        @pl.when(mod(y - n + NY, NY) != z)
        def _():
            remote(zs.at[n], zr.at[0], zsend.at[n], zrecv.at[0], at_z(1)).wait_send()

    @pl.when(side != c)
    def _():
        for k in range(NZ):
            remote(
                zg.at[here], obuf.at[c, here, place], osend.at[k, 0], orecv.at[0, 0, 0], partner
            ).wait_send()

    final.wait()


def on_device(acts, gate, up, down, shrink, expand, row_adapter, page_table):
    batches, rows, width = acts.shape
    hidden = gate.shape[1]
    out_width = down.shape[1]
    pages, rank, _ = shrink.shape
    rank_local, ff = expand.shape[1:]
    piece = rows // NY
    cols = 2 * out_width // NX
    anyspec = pl.BlockSpec(memory_space=pl.ANY)
    dma = pltpu.SemaphoreType.DMA
    ranks = 2 * rank_local
    scratch = [
        pltpu.VMEM(row_adapter.shape, jnp.int32),
        pltpu.VMEM((1, page_table.shape[0]), jnp.int32),
        pltpu.VMEM((2, rows, width), BF16),
        pltpu.VMEM((rows, width), BF16),
        pltpu.VMEM((width, hidden), BF16),
        pltpu.VMEM((width, hidden), BF16),
        pltpu.VMEM((width, hidden), BF16),
        pltpu.VMEM((width, hidden), BF16),
        pltpu.VMEM((2, hidden, out_width), BF16),
        pltpu.VMEM((pages, rank, width), BF16),
        pltpu.VMEM((pages, rank_local, ff), BF16),
        pltpu.VMEM((2, rank_local, ff), BF16),
        pltpu.VMEM((rank_local, ff), BF16),
        pltpu.VMEM((ranks, ff), BF16),
        pltpu.VMEM((NPOOL, ranks, hidden), BF16),
        pltpu.VMEM((NPOOL, ranks, rows), BF16),
        pltpu.VMEM((rank, rows), F32),
        pltpu.VMEM((rank, rows), F32),
        pltpu.VMEM((NY, ranks, rows), F32),
        pltpu.VMEM((NY, ranks, rows), F32),
        pltpu.VMEM((2, ranks, rows), BF16),
        pltpu.VMEM((NX, ranks, rows), BF16),
        pltpu.VMEM((NZ, ranks, rows), BF16),
        pltpu.VMEM((rows, hidden), F32),
        pltpu.VMEM((rows, hidden), F32),
        pltpu.VMEM((NY, piece, hidden), BF16),
        pltpu.VMEM((NY, piece, hidden), BF16),
        pltpu.VMEM((piece, hidden), F32),
        pltpu.VMEM((2, 2, 2, piece // 4, hidden), BF16),
        pltpu.VMEM((2, 2, 2, piece // 2, hidden), BF16),
        pltpu.VMEM((2, 2, piece, hidden), BF16),
        pltpu.VMEM((2, 2, 2, piece // 2, hidden), BF16),
        pltpu.VMEM((NY, piece, hidden), BF16),
        pltpu.VMEM((NY, NX, piece, cols), BF16),
        pltpu.VMEM((NY, NX, piece, cols), BF16),
        pltpu.VMEM((NY, piece, cols), BF16),
        pltpu.VMEM((NZ, piece, cols), BF16),
        pltpu.VMEM((rows, cols), BF16),
        pltpu.VMEM((batches, rows, out_width), BF16),
        dma((9,)),
        dma((6,)), dma((6,)),
        dma((NPOOL,)), dma((NPOOL,)),
        dma((NY,)), dma((NY,)),
        dma((NX,)), dma((NX,)),
        dma((NZ,)), dma((NZ,)),
        dma((2, 5, 2, 2)), dma((2, 5, 2, 2)),
        dma((4, 2, 2)), dma((4, 2, 2)),
        dma((NY, NX)), dma((NY, NX)),
        dma((NY,)), dma((NZ,)),
        dma((NZ,)), dma((NZ,)),
        dma((NZ, NX)), dma((2, 2, NZ)),
    ]
    return pl.pallas_call(
        kernel,
        out_shape=jax.ShapeDtypeStruct((batches, rows, out_width), BF16),
        in_specs=[anyspec] * 8,
        out_specs=anyspec,
        scratch_shapes=scratch,
        compiler_params=pltpu.CompilerParams(
            collective_id=0, has_side_effects=True, vmem_limit_bytes=VMEM_LIMIT
        ),
        name="layer",
    )(*[pltpu.with_memory_space_constraint(v, pltpu.HBM) for v in (acts, gate, up, down, shrink, expand, row_adapter, page_table.reshape(1, -1))])


def solution(mesh):
    return jax.shard_map(
        on_device,
        mesh=mesh,
        in_specs=(
            P(None, None, "tp"),
            P("tp", "pool"),
            P("tp", "pool"),
            P("pool", "tp"),
            P("pool", None, "tp"),
            P("pool", "tp", None),
            P(),
            P(),
        ),
        out_specs=P(None, None, "tp"),
        check_vma=False,
    )
```
